512 devices in a mesh: tile: 16 (over x, y_hi, core), orient: 32 (over z, y_lo).
Axes of the slice: x: 4, y: 4 (y_hi: 2, y_lo: 2; y = y_hi * 2 + y_lo), z: 16, core: 2. Of those that a mesh axis runs over, the one named last changes fastest.
Arguments:
- micrograph: bfloat16 [4096, 512], P('tile'), may hold values from -140 to 140
- templates: bfloat16 [64, 384, 384], P('orient', 'tile'), may hold values from -6 to 6
- defocus: float32 [4], replicated, may hold values from 8 to 40
- group_of_tile: int32 [16], P('tile'), may hold values from 0 to 3
Outputs:
- top_score: float32 [4096, 128], P(('tile', 'orient'))
- zscore: float32 [4096, 128], P(('tile', 'orient'))
The draws below stay inside these ranges and needn't reach their ends.
All inputs are finite; a program needn't handle non-finite values.
Results may differ from the reference program's by a relative error of at most 0.0085.
Values may be sent and summed in bfloat16 or wider, within the bound.
A program may use at most 64 MiB of HBM per device.

```python
import math
import jax
import jax.numpy as jnp
from jax import lax

TS = 384
STRIP = 256
OUTC = 128
GROUPS = 4
ROWS = 4096
LROW = 640
LCOL = 512
ORIENTS = 64
N_TILE = 16


def draw_micrograph(key, part):
    row_key, col_key, pixel_key = jax.random.split(key, 3)
    row_count = STRIP * N_TILE
    col_count = OUTC + TS
    position = jnp.arange(row_count, dtype=jnp.float32) / row_count
    row_scale = jnp.exp(jnp.log(3.0) * position + jnp.log(3.0) * jax.random.uniform(row_key, (row_count,), jnp.float32))
    col_scale = jnp.exp(jnp.log(3.0) * jax.random.uniform(col_key, (col_count,), jnp.float32))
    pixels = jnp.clip(jax.random.normal(pixel_key, (row_count, col_count), jnp.float32), -5.0, 5.0)
    return (pixels * row_scale[:, None] * col_scale[None, :]).astype(jnp.bfloat16)


def plant(drawn, rng, smallest, high):
    dims = drawn.shape
    place = [jax.random.randint(jax.random.fold_in(rng, axis), (), 0, dims[axis]) for axis in range(len(dims))]
    drawn = drawn.at[tuple(place)].set(smallest)
    longest = dims.index(max(dims))
    place[longest] = (place[longest] + 1) % dims[longest]
    return drawn.at[tuple(place)].set(high)


def levels(stream_key, extent, pieces, smallest, largest):
    factor_of = 1.0
    for dim, parts in pieces:
        steps = jax.random.uniform(jax.random.fold_in(jax.random.fold_in(stream_key, 6), dim), (parts,), jnp.float32, smallest / len(pieces), largest / len(pieces))
        factor_of = factor_of * jnp.repeat(jnp.exp(steps), extent[dim] // parts).reshape((-1,) + (1,) * (len(extent) - 1 - dim))
    return factor_of


def gaussian(key, extent, spread, most, cuts=(), held_as=jnp.bfloat16):
    entries = spread * jax.random.normal(key, extent, jnp.float32)
    if cuts:
        entries = entries * levels(key, extent, cuts, -0.22, 0.18)
    return jnp.clip(entries, -most, most).astype(held_as)


def setup_inputs(seed: int = 0) -> dict:
    keys = jax.random.split(jax.random.key(seed), 5)
    return {
        "micrograph": draw_micrograph(jax.random.fold_in(keys[4], 71), 0),
        "templates": gaussian(keys[1], (ORIENTS, TS, TS), 1.0, 6.0, ((0, 32), (1, 16))),
        "defocus": jnp.clip(jnp.exp(jax.random.uniform(keys[2], (GROUPS,), jnp.float32, math.log(8.0), math.log(40.0))), 8.0, 40.0),
        "group_of_tile": plant(jax.random.randint(keys[3], (N_TILE,), 0, GROUPS), jax.random.fold_in(keys[3], 1), 0, GROUPS - 1).astype(jnp.int32),
    }


def twiddle(row_count, col_count, modulus, sign_value):
    freq_index = jnp.arange(row_count, dtype=jnp.int32)[:, None]
    place_index = jnp.arange(col_count, dtype=jnp.int32)[None, :]
    residue = freq_index * place_index % modulus
    mirrored = modulus - residue
    lowest = jnp.minimum(residue, mirrored)
    flipped = jnp.where(residue > mirrored, -1.0, 1.0).astype(jnp.float32)
    angle = lowest.astype(jnp.float32) * jnp.float32(2.0 * math.pi / modulus)
    return (jnp.cos(angle).astype(jnp.bfloat16), (sign_value * flipped * jnp.sin(angle)).astype(jnp.bfloat16))

def quarter_turn(stacked):
    middle = stacked.shape[-1] // 2
    return jnp.concatenate([-stacked[..., middle:], stacked[..., :middle]], axis=-1)

def rotate_apply(table_cos, table_sin, stacked):
    return jnp.dot(table_cos, stacked, preferred_element_type=jnp.float32) + jnp.dot(table_sin, quarter_turn(stacked), preferred_element_type=jnp.float32)

def signed_freq(length):
    index = jnp.arange(length, dtype=jnp.int32)
    return jnp.where(2 * index < length, index, index - length).astype(jnp.float32) / length

def ctf_table(defocus_value):
    row_freq = signed_freq(LROW)
    col_freq = signed_freq(LCOL)
    radius = row_freq[:, None] ** 2 + col_freq[None, :] ** 2
    return -jnp.sin(jnp.float32(math.pi) * defocus_value * radius + 0.07)

def reference(micrograph, templates, defocus, group_of_tile):
    col_cos, col_sin = twiddle(LCOL, LCOL, LCOL, -1.0)
    col_table = jnp.concatenate([col_cos, col_sin], axis=1)
    row_cos, row_sin = twiddle(LROW, LROW, LROW, -1.0)
    back_cos, back_sin = twiddle(LCOL, OUTC, LCOL, 1.0)
    back_table = jnp.concatenate([jnp.concatenate([back_cos, back_sin], 1), jnp.concatenate([-back_sin, back_cos], 1)], 0)
    out_cos, out_sin = twiddle(STRIP, LROW, LROW, 1.0)
    padded = jnp.concatenate([micrograph, jnp.zeros((2 * STRIP, LCOL), jnp.bfloat16)], 0)

    def spectrum(tile_index):
        window = lax.dynamic_slice_in_dim(padded, tile_index * STRIP, LROW, 0)
        column_part = jnp.dot(window, col_table, preferred_element_type=jnp.float32).astype(jnp.bfloat16)
        return rotate_apply(row_cos, row_sin, column_part)
    spectra = lax.map(spectrum, jnp.arange(N_TILE, dtype=jnp.int32))
    power_map = lax.optimization_barrier(jnp.sum(spectra[..., :LCOL] ** 2 + spectra[..., LCOL:] ** 2, axis=0)) / N_TILE
    whiten = lax.rsqrt(power_map + jnp.mean(power_map))
    whiten_both = jnp.concatenate([whiten, whiten], axis=1)
    widened = templates.astype(jnp.float32)
    tpl_spec = jnp.einsum('abc,cd->abd', widened, col_table[:TS].astype(jnp.float32)).astype(jnp.bfloat16)
    sums = lax.optimization_barrier(jnp.sum(widened, axis=(1, 2)))
    squares = lax.optimization_barrier(jnp.sum(widened * widened, axis=(1, 2)))
    mean_tpl = sums / (TS * TS)
    spread_tpl = jnp.sqrt(squares / (TS * TS) - mean_tpl * mean_tpl + 1e-05)
    raw_spec = lax.map(lambda single: rotate_apply(row_cos[:, :TS], row_sin[:, :TS], single), tpl_spec)
    row_sum_cos = lax.optimization_barrier(jnp.sum(row_cos[:, :TS].astype(jnp.float32), axis=1))
    row_sum_sin = lax.optimization_barrier(jnp.sum(row_sin[:, :TS].astype(jnp.float32), axis=1))
    col_sums = lax.optimization_barrier(jnp.sum(col_table[:TS].astype(jnp.float32), axis=0))
    col_sum_cos = col_sums[:LCOL]
    col_sum_sin = col_sums[LCOL:]
    box = jnp.concatenate([row_sum_cos[:, None] * col_sum_cos[None, :] - row_sum_sin[:, None] * col_sum_sin[None, :], row_sum_cos[:, None] * col_sum_sin[None, :] + row_sum_sin[:, None] * col_sum_cos[None, :]], axis=1)

    def per_tile(tile_index):
        weighted = spectra[tile_index] * whiten_both
        ctf_map = ctf_table(defocus[group_of_tile[tile_index]])
        image_re = weighted[:, :LCOL]
        image_im = weighted[:, LCOL:]

        def per_template(running, inputs):
            raw_single, mean_single, spread_single = inputs
            shaped = (raw_single - mean_single * box) / spread_single
            shape_re = shaped[:, :LCOL]
            shape_im = shaped[:, LCOL:]
            product = jnp.concatenate([(image_re * shape_re + image_im * shape_im) * ctf_map, (image_im * shape_re - image_re * shape_im) * ctf_map], axis=1).astype(jnp.bfloat16)
            partial_back = jnp.dot(product, back_table, preferred_element_type=jnp.float32).astype(jnp.bfloat16)
            score = (jnp.dot(out_cos, partial_back[:, :OUTC], preferred_element_type=jnp.float32) - jnp.dot(out_sin, partial_back[:, OUTC:], preferred_element_type=jnp.float32)) / (LROW * LCOL)
            best, score_sum, score_squares = running
            return ((jnp.maximum(best, score), score_sum + score, score_squares + score * score), None)
        start_state = (jnp.full((STRIP, OUTC), -jnp.inf, jnp.float32), jnp.zeros((STRIP, OUTC), jnp.float32), jnp.zeros((STRIP, OUTC), jnp.float32))
        final_state, _ = lax.scan(per_template, start_state, (raw_spec, mean_tpl, spread_tpl))
        return final_state
    best, score_sum, score_squares = lax.map(per_tile, jnp.arange(N_TILE, dtype=jnp.int32))
    best = best.reshape(ROWS, OUTC)
    score_mean = score_sum.reshape(ROWS, OUTC) / ORIENTS
    score_var = score_squares.reshape(ROWS, OUTC) / ORIENTS - score_mean * score_mean
    return (best, (best - score_mean) / jnp.sqrt(score_var + 1e-05))
```

```python
import functools
import math

import jax
import jax.numpy as jnp
import numpy as np
from jax import lax
from jax.experimental import pallas as pl
from jax.experimental.pallas import tpu as pltpu
from jax.sharding import PartitionSpec as P

TS, STRIP, OUTC, LROW, LCOL = 384, 256, 128, 640, 512
KH = 336
KP = 384
BLK = 128
NQ = LCOL // BLK
CHIPS = 8
KC = KP // CHIPS
MESH = pl.DeviceIdType.MESH
BF, F32 = jnp.bfloat16, jnp.float32


def twiddle(rows, cols, modulus, sign):
    residue = np.arange(rows)[:, None] * np.arange(cols)[None, :] % modulus
    mirrored = modulus - residue
    angle = np.minimum(residue, mirrored).astype(np.float32) * np.float32(2 * math.pi / modulus)
    flipped = np.where(residue > mirrored, -1.0, 1.0).astype(np.float32)
    return np.cos(angle).astype(BF), (np.float32(sign) * flipped * np.sin(angle)).astype(BF)


def tables():
    cc, cs = twiddle(LCOL, LCOL, LCOL, -1.0)
    col = np.stack(
        [
            np.concatenate([cc[:, q * BLK : (q + 1) * BLK], cs[:, q * BLK : (q + 1) * BLK]], 1)
            for q in range(NQ)
        ]
    )
    col_sum = col[:, :TS].astype(np.float32).sum(1, keepdims=True)
    rc, rs = twiddle(LROW, LROW, LROW, -1.0)
    rows = np.zeros((2 * KH, LROW), BF)
    half = LROW // 2 + 1
    rows[:half], rows[KH : KH + half] = rc[:half], rs[:half]
    bc, bs = twiddle(LCOL, OUTC, LCOL, 1.0)
    back = np.concatenate(
        [
            np.block(
                [
                    [bc[q * BLK : (q + 1) * BLK], bs[q * BLK : (q + 1) * BLK]],
                    [-bs[q * BLK : (q + 1) * BLK], bc[q * BLK : (q + 1) * BLK]],
                ]
            )
            for q in range(NQ)
        ]
    ).astype(BF)
    ac, as_ = twiddle(STRIP, LROW, LROW, 1.0)
    weight = np.full(half, 2.0, np.float32)
    weight[0] = weight[-1] = 1.0
    out = np.zeros((STRIP, 2 * KH), np.float32)
    out[:, :half] = weight * ac[:, :half].astype(np.float32)
    out[:, KH : KH + half] = -weight * as_[:, :half].astype(np.float32)
    return rows, col, back, out.astype(BF), col_sum


def combine(product, n=KH):
    real = product[:n, :BLK] - product[n:, BLK:]
    imag = product[:n, BLK:] + product[n:, :BLK]
    return real, imag


def kernel(
    mic, tpl, defo, group, rows_h, col_h, back_h, out_h, col_sum,
    top_o, z_o,
    rows, col, back, outt, frame, cspec, spec, ybuf, tg, tr, tf, tspec, hsp,
    psend, pown, precv, comb, rsb, gall, ctf_s, ctf_c, qb, ys, sbuf, rbuf,
    lsem, ssem, rsem, asem, bsem,
):
    t, o = lax.axis_index("tile"), lax.axis_index("orient")
    z, ylo = o // 2, o % 2
    j, c = t // 2, t % 2
    x, yh = j // 2, j % 2
    other = 1 - c

    def orient_at(tile):
        return z * 2 + (ylo + yh + (tile // 2) % 2) % 2

    def near(tile):
        return (tile, orient_at(tile))

    loads = [
        pltpu.make_async_copy(mic, frame.at[pl.ds(0, STRIP)], lsem.at[0]),
        pltpu.make_async_copy(col_h, col, lsem.at[1]),
        pltpu.make_async_copy(rows_h, rows, lsem.at[2]),
        pltpu.make_async_copy(back_h, back, lsem.at[3]),
        pltpu.make_async_copy(out_h, outt, lsem.at[4]),
        pltpu.make_async_copy(tpl.at[c], tg.at[t], lsem.at[5]),
    ]
    for copy in loads:
        copy.start()

    barrier = pltpu.get_barrier_semaphore()

    def greet(device):
        pl.semaphore_signal(barrier, inc=1, device_id=device, device_id_type=MESH)

    def orient_peer(d):
        return (t, lax.rem(o + d, 32))

    def greet_orient(d, carry):
        greet(orient_peer(d))
        return carry

    for d in (1, 2, 14, 15):
        greet(near(lax.rem(t + d, 16)))
    ty = x * 4 + (1 - yh) * 2 + c
    greet((ty, o))
    partner = (j * 2 + other, o)
    greet(partner)
    for dx in (1, 2, 3):
        for core in (0, 1):
            greet((lax.rem(x + dx, 4) * 4 + yh * 2 + core, o))
    for d in range(1, CHIPS):
        greet(near(lax.rem(j + d, CHIPS) * 2 + c))
    lax.fori_loop(1, 32, greet_orient, 0)

    started = []

    def remote(src, dst, send, recv, device):
        return pltpu.make_async_remote_copy(
            src_ref=src, dst_ref=dst, send_sem=send, recv_sem=recv, device_id=device, device_id_type=MESH
        )

    def send(src, dst, index, recv_index, device):
        copy = remote(src, dst, ssem.at[index], rsem.at[recv_index], device)
        copy.start()
        started.append(copy)

    def arrive(dst, index):
        remote(dst, dst, ssem.at[0], rsem.at[index], partner).wait_recv()

    loads[0].wait()
    loads[1].wait()
    for q in range(NQ):
        cspec[q, 0:STRIP, :] = jnp.dot(
            frame[0:STRIP, :], col[q], preferred_element_type=F32
        ).astype(BF)

    pl.semaphore_wait(barrier, 4 + 1 + 1 + 6 + 7 + 31)

    t1, t2 = lax.rem(t + 15, 16), lax.rem(t + 14, 16)
    send(mic, frame.at[pl.ds(STRIP, STRIP)], 0, 0, near(t1))
    send(mic.at[pl.ds(0, BLK)], frame.at[pl.ds(2 * STRIP, BLK)], 1, 1, near(t2))
    send(tpl, ybuf, 2, 2, (ty, o))

    chosen = group[0]
    depth = jnp.float32(0.0)
    for g in range(4):
        depth = depth + jnp.where(chosen == g, defo[g], 0.0)
    depth = depth * jnp.float32(math.pi)
    k = lax.broadcasted_iota(jnp.int32, (KH, BLK), 0).astype(F32) / LROW
    angle = depth * (k * k) + 0.07
    ctf_s[...] = jnp.sin(angle)
    ctf_c[...] = jnp.cos(angle)

    arrive(ybuf, 2)
    fill = pltpu.make_async_copy(ybuf.at[c], tg.at[ty], lsem.at[6])
    fill.start()
    at = 3
    for dx in (1, 2, 3):
        xd = lax.rem(x + dx, 4)
        for core in (0, 1):
            for piece in (0, 1):
                src = tpl.at[core] if piece == 0 else ybuf.at[core]
                slot = t if piece == 0 else ty
                send(
                    src, tg.at[slot], at, 3 + (dx - 1) * 4 + c * 2 + piece,
                    (xd * 4 + yh * 2 + core, o),
                )
                at += 1
    send(tpl.at[other], tg.at[t], 15, 15, partner)
    send(ybuf.at[other], tg.at[ty], 16, 16, partner)

    arrive(frame.at[pl.ds(STRIP, STRIP)], 0)
    arrive(frame.at[pl.ds(2 * STRIP, BLK)], 1)
    keep1 = jnp.where(t < 15, 1.0, 0.0).astype(F32)
    keep2 = jnp.where(t < 14, 1.0, 0.0).astype(F32)
    row = lax.broadcasted_iota(jnp.int32, (TS, 2 * BLK), 0)
    keep = jnp.where(row < STRIP, keep1, keep2)
    for q in range(NQ):
        part = jnp.dot(frame[STRIP:LROW, :], col[q], preferred_element_type=F32)
        cspec[q, STRIP:LROW, :] = (part * keep).astype(BF)
    loads[2].wait()

    def spectrum(q):
        real, imag = combine(jnp.dot(rows[...], cspec[q], preferred_element_type=F32))
        spec[q, :, 0:BLK] = real
        spec[q, :, BLK:] = imag
        return real * real + imag * imag

    for i in range(2):
        psend[i] = spectrum(2 * other + i).astype(BF)
    send(psend, precv, 17, 17, partner)
    for i in range(2):
        pown[i, 0:KH, :] = spectrum(2 * c + i)
        pown[i, KH:KP, :] = jnp.zeros((KP - KH, BLK), F32)

    for dx in (1, 2, 3):
        xs = lax.rem(x + 4 - dx, 4)
        for core in (0, 1):
            for piece in (0, 1):
                row_of = yh if piece == 0 else 1 - yh
                arrive(tg.at[xs * 4 + row_of * 2 + core], 3 + (dx - 1) * 4 + core * 2 + piece)
    arrive(tg.at[j * 2 + other], 15)
    arrive(tg.at[x * 4 + (1 - yh) * 2 + other], 16)
    loads[5].wait()
    fill.wait()
    send(tg, tr, 18, 18, partner)

    arrive(precv, 17)
    for i in range(2):
        pown[i, 0:KH, :] = pown[i, 0:KH, :] + precv[i].astype(F32)
        for n in range(CHIPS):
            comb[n, i] = pown[i, n * KC : (n + 1) * KC, :].astype(BF)
    for d in range(1, CHIPS):
        to = lax.rem(j + d, CHIPS)
        send(comb.at[to], rsb.at[d - 1], 18 + d, 18 + d, near(to * 2 + c))

    arrive(tr, 18)
    for n, held in enumerate((tg, tr)):
        for s in range(16):
            tf[s * 24 : (s + 1) * 24, :] = held[s].astype(F32)
        values = tf[...]
        mean = jnp.sum(values) / (TS * TS)
        spread = jnp.sum(values * values) / (TS * TS) - mean * mean + 1e-05
        inverse = lax.rsqrt(jnp.full((1, 2 * BLK), spread, F32)) / (LROW * LCOL)
        rounded = values.astype(BF)
        for q in range(NQ):
            part = jnp.dot(rounded, col[q, 0:TS, :], preferred_element_type=F32)
            tspec[n, q] = ((part - mean * col_sum[q]) * inverse).astype(BF)

    for d in range(1, CHIPS):
        arrive(rsb.at[d - 1], 18 + d)
    total = comb[j].astype(F32)
    for d in range(1, CHIPS):
        total = total + rsb[d - 1].astype(F32)
    gall[c, j] = total.astype(BF)
    for d in range(1, CHIPS):
        to = lax.rem(j + d, CHIPS)
        send(gall.at[c, j], gall.at[c, j], 25 + d, 25 + d, near(to * 2 + c))

    for n in range(2):
        for q in range(NQ):
            real, imag = combine(
                jnp.dot(rows[:, 0:TS], tspec[n, q], preferred_element_type=F32)
            )
            hsp[n, q, :, 0:BLK] = real
            hsp[n, q, :, BLK:] = imag

    for d in range(1, CHIPS):
        arrive(gall.at[c, lax.rem(j + CHIPS - d, CHIPS)], 25 + d)
    send(gall.at[c], gall.at[c], 33, 33, partner)
    arrive(gall.at[other], 33)

    def power(q):
        return jnp.concatenate([gall[q // 2, n, q % 2].astype(F32) for n in range(CHIPS)], 0)

    k = lax.broadcasted_iota(jnp.int32, (KP, BLK), 0)
    weight = jnp.where(k < LROW // 2, 2.0, 1.0) * jnp.where(k <= LROW // 2, 1.0, 0.0)
    weight = jnp.where(k == 0, 1.0, weight)
    summed = jnp.zeros((KP, BLK), F32)
    for q in range(NQ):
        summed = summed + power(q)
    average = jnp.sum(summed * weight) / (LROW * LCOL * 16.0)
    for q in range(NQ):
        lane = lax.broadcasted_iota(jnp.int32, (1, BLK), 1) + q * BLK
        lane = jnp.where(2 * lane < LCOL, lane, lane - LCOL).astype(F32) / LCOL
        phase = depth * (lane * lane)
        factor = -(ctf_s[...] * jnp.cos(phase) + ctf_c[...] * jnp.sin(phase))
        factor = factor * lax.rsqrt(power(q)[0:KH] / 16.0 + average)
        real, imag = spec[q, :, 0:BLK] * factor, spec[q, :, BLK:] * factor
        for n in range(2):
            h_re, h_im = hsp[n, q, :, 0:BLK], hsp[n, q, :, BLK:]
            qb[n * KH : (n + 1) * KH, q * 256 : q * 256 + BLK] = (real * h_re + imag * h_im).astype(BF)
            qb[n * KH : (n + 1) * KH, q * 256 + BLK : (q + 1) * 256] = (imag * h_re - real * h_im).astype(BF)
    loads[3].wait()
    loads[4].wait()
    for n in range(2):
        y = jnp.dot(
            qb[n * KH : (n + 1) * KH, :], back[...], preferred_element_type=F32
        ).astype(BF)
        ys[0:KH, n * BLK : (n + 1) * BLK] = y[:, 0:BLK]
        ys[KH:, n * BLK : (n + 1) * BLK] = y[:, BLK:]
    score = jnp.dot(outt[...], ys[...], preferred_element_type=F32)
    for n in range(32):
        block = score[n * 8 : (n + 1) * 8, :]
        sbuf[n] = jnp.concatenate([block[:, 0:BLK], block[:, BLK:]], 0).astype(BF)

    def a2a(d):
        to = lax.rem(o + d, 32)
        return remote(sbuf.at[to], rbuf.at[o], asem.at[d], bsem.at[d], (t, to))

    def a2a_start(d, carry):
        a2a(d).start()
        return carry

    def a2a_wait(d, carry):
        src = lax.rem(o + 32 - d, 32)
        remote(rbuf.at[src], rbuf.at[src], asem.at[d], bsem.at[d], partner).wait_recv()
        return carry

    def a2a_sent(d, carry):
        a2a(d).wait_send()
        return carry

    lax.fori_loop(1, 32, a2a_start, 0)
    keep_own = pltpu.make_async_copy(sbuf.at[o], rbuf.at[o], lsem.at[7])
    keep_own.start()
    for copy in started:
        copy.wait_send()
    keep_own.wait()
    lax.fori_loop(1, 32, a2a_wait, 0)
    best = jnp.full((8, BLK), -jnp.inf, F32)
    first = jnp.zeros((8, BLK), F32)
    second = jnp.zeros((8, BLK), F32)
    for n in range(32):
        pair = rbuf[n].astype(F32)
        a, b = pair[0:8], pair[8:16]
        best = jnp.maximum(best, jnp.maximum(a, b))
        first = first + (a + b)
        second = second + (a * a + b * b)
    mean = first / 64.0
    spread = second / 64.0 - mean * mean
    top_o[...] = best
    z_o[...] = (best - mean) / jnp.sqrt(spread + 1e-05)
    lax.fori_loop(1, 32, a2a_sent, 0)


def local(consts, micrograph, templates, defocus, group_of_tile):
    rows, col, back, out, col_sum = consts
    hbm = pl.BlockSpec(memory_space=pl.ANY)
    vmem = pl.BlockSpec(memory_space=pltpu.VMEM)
    smem = pl.BlockSpec(memory_space=pltpu.SMEM)
    v = pltpu.VMEM
    return pl.pallas_call(
        kernel,
        out_shape=(jax.ShapeDtypeStruct((8, OUTC), F32),) * 2,
        in_specs=[hbm, hbm, smem, smem, hbm, hbm, hbm, hbm, vmem],
        out_specs=(vmem, vmem),
        scratch_shapes=[
            v((2 * KH, LROW), BF),
            v((NQ, LCOL, 2 * BLK), BF),
            v((2 * LCOL, 2 * OUTC), BF),
            v((STRIP, 2 * KH), BF),
            v((LROW, LCOL), BF),
            v((NQ, LROW, 2 * BLK), BF),
            v((NQ, KH, 2 * BLK), F32),
            v((2, 24, TS), BF),
            v((16, 24, TS), BF),
            v((16, 24, TS), BF),
            v((TS, TS), F32),
            v((2, NQ, TS, 2 * BLK), BF),
            v((2, NQ, KH, 2 * BLK), F32),
            v((2, KH, BLK), BF),
            v((2, KP, BLK), F32),
            v((2, KH, BLK), BF),
            v((CHIPS, 2, KC, BLK), BF),
            v((CHIPS - 1, 2, KC, BLK), BF),
            v((2, CHIPS, 2, KC, BLK), BF),
            v((KH, BLK), F32),
            v((KH, BLK), F32),
            v((2 * KH, 2 * LCOL), BF),
            v((2 * KH, 2 * BLK), BF),
            v((32, 16, BLK), BF),
            v((32, 16, BLK), BF),
            pltpu.SemaphoreType.DMA((8,)),
            pltpu.SemaphoreType.DMA((34,)),
            pltpu.SemaphoreType.DMA((34,)),
            pltpu.SemaphoreType.DMA((32,)),
            pltpu.SemaphoreType.DMA((32,)),
        ],
        compiler_params=pltpu.CompilerParams(collective_id=0, has_side_effects=True),
        name="match",
    )(micrograph, templates, defocus, group_of_tile, rows, col, back, out, col_sum)


def solution(mesh):
    consts = tuple(jnp.asarray(a) for a in tables())
    return jax.shard_map(
        functools.partial(local, consts),
        mesh=mesh,
        in_specs=(P("tile", None), P("orient", "tile", None), P(), P("tile")),
        out_specs=(P(("tile", "orient"), None),) * 2,
        check_vma=False,
    )
```

```python
import functools
import math

import jax
import jax.numpy as jnp
import numpy as np
from jax import lax
from jax.experimental import pallas as pl
from jax.experimental.pallas import tpu as pltpu
from jax.sharding import PartitionSpec as P

TS, STRIP, OUTC, LROW, LCOL = 384, 256, 128, 640, 512
KH = 336
KP = 384
BLK = 128
NQ = LCOL // BLK
CHIPS = 8
KC = KP // CHIPS
FAR_FIRST = (3, 5, 4, 2, 6, 1, 7)
MESH = pl.DeviceIdType.MESH
BF, F32 = jnp.bfloat16, jnp.float32


def twiddle(rows, cols, modulus, sign):
    residue = np.arange(rows)[:, None] * np.arange(cols)[None, :] % modulus
    mirrored = modulus - residue
    angle = np.minimum(residue, mirrored).astype(np.float32) * np.float32(2 * math.pi / modulus)
    flipped = np.where(residue > mirrored, -1.0, 1.0).astype(np.float32)
    return np.cos(angle).astype(BF), (np.float32(sign) * flipped * np.sin(angle)).astype(BF)


def tables():
    cc, cs = twiddle(LCOL, LCOL, LCOL, -1.0)
    col = np.stack(
        [
            np.concatenate([cc[:, q * BLK : (q + 1) * BLK], cs[:, q * BLK : (q + 1) * BLK]], 1)
            for q in range(NQ)
        ]
    )
    col_sum = col[:, :TS].astype(np.float32).sum(1, keepdims=True)
    rc, rs = twiddle(LROW, LROW, LROW, -1.0)
    rows = np.zeros((2 * KH, LROW), BF)
    half = LROW // 2 + 1
    rows[:half], rows[KH : KH + half] = rc[:half], rs[:half]
    bc, bs = twiddle(LCOL, OUTC, LCOL, 1.0)
    back = np.concatenate(
        [
            np.block(
                [
                    [bc[q * BLK : (q + 1) * BLK], bs[q * BLK : (q + 1) * BLK]],
                    [-bs[q * BLK : (q + 1) * BLK], bc[q * BLK : (q + 1) * BLK]],
                ]
            )
            for q in range(NQ)
        ]
    ).astype(BF)
    ac, as_ = twiddle(STRIP, LROW, LROW, 1.0)
    weight = np.full(half, 2.0, np.float32)
    weight[0] = weight[-1] = 1.0
    out = np.zeros((STRIP, 2 * KH), np.float32)
    out[:, :half] = weight * ac[:, :half].astype(np.float32)
    out[:, KH : KH + half] = -weight * as_[:, :half].astype(np.float32)
    return rows, col, back, out.astype(BF), col_sum


def combine(product, n=KH):
    real = product[:n, :BLK] - product[n:, BLK:]
    imag = product[:n, BLK:] + product[n:, :BLK]
    return real, imag


def kernel(
    mic, tpl, defo, group, rows_h, col_h, back_h, out_h, col_sum,
    res_o,
    rows, col, back, outt, frame, cspec, spec, ybuf, tg, tr, tf, tspec, hsp,
    psend, pown, precv, comb, rsb, gall, ctf_s, ctf_c, qb, ys, sbuf, rbuf,
    lsem, ssem, rsem, asem, bsem, esem,
):
    t, o = lax.axis_index("tile"), lax.axis_index("orient")
    z, ylo = o // 2, o % 2
    j, c = t // 2, t % 2
    x, yh = j // 2, j % 2
    other = 1 - c

    def orient_at(tile):
        return z * 2 + (ylo + yh + (tile // 2) % 2) % 2

    def near(tile):
        return (tile, orient_at(tile))

    loads = [
        pltpu.make_async_copy(mic, frame.at[pl.ds(0, STRIP)], lsem.at[0]),
        pltpu.make_async_copy(col_h, col, lsem.at[1]),
        pltpu.make_async_copy(rows_h, rows, lsem.at[2]),
        pltpu.make_async_copy(back_h, back, lsem.at[3]),
        pltpu.make_async_copy(out_h, outt, lsem.at[4]),
        pltpu.make_async_copy(tpl.at[c], tg.at[t], lsem.at[5]),
    ]
    for copy in loads:
        copy.start()

    barrier = pltpu.get_barrier_semaphore()

    def greet(device):
        pl.semaphore_signal(barrier, inc=1, device_id=device, device_id_type=MESH)

    def orient_peer(d):
        return (t, lax.rem(o + d, 32))

    beside = near(lax.rem(j + CHIPS + 2 * c - 1, CHIPS) * 2 + other)
    greet(beside)
    for d in (1, 31):
        greet(orient_peer(d))
    ty = x * 4 + (1 - yh) * 2 + c
    greet((ty, o))
    partner = (j * 2 + other, o)
    greet(partner)
    for dx in (1, 2, 3):
        for core in (0, 1):
            greet((lax.rem(x + dx, 4) * 4 + yh * 2 + core, o))
    for d in range(1, CHIPS):
        greet(near(lax.rem(j + d, CHIPS) * 2 + c))

    started = []

    def remote(src, dst, send, recv, device):
        return pltpu.make_async_remote_copy(
            src_ref=src, dst_ref=dst, send_sem=send, recv_sem=recv, device_id=device, device_id_type=MESH
        )

    def send(src, dst, index, recv_index, device):
        copy = remote(src, dst, ssem.at[index], rsem.at[recv_index], device)
        copy.start()
        started.append(copy)

    def arrive(dst, index):
        remote(dst, dst, ssem.at[0], rsem.at[index], partner).wait_recv()

    def tell(r):
        step = max(1, 2 ** (r - 1))
        for d in (step, 32 - step):
            pl.semaphore_signal(
                esem.at[r - 1], inc=1, device_id=orient_peer(d), device_id_type=MESH
            )

    def told(r):
        pl.semaphore_wait(esem.at[r - 1], 2)

    pl.semaphore_wait(barrier, 1 + 2 + 1 + 1 + 6 + 7)

    before = lax.rem(j + CHIPS - 1, CHIPS)
    across = near(before * 2 + 1)
    last = c == 1
    first_rows, second_rows = mic.at[pl.ds(0, BLK)], mic.at[pl.ds(BLK, BLK)]
    send(
        first_rows, frame.at[pl.ds(pl.multiple_of(STRIP + STRIP * c, STRIP), BLK)],
        0, 35 + 2 * c, across,
    )
    there = (jnp.where(last, j, before) * 2 + other, jnp.where(last, o, across[1]))
    send(second_rows, frame.at[pl.ds(STRIP + BLK, BLK)], 1, 36, there)
    inner = [
        remote(first_rows, frame.at[pl.ds(STRIP, BLK)], ssem.at[34], rsem.at[35], partner),
        remote(
            frame.at[pl.ds(STRIP, BLK)], frame.at[pl.ds(2 * STRIP, BLK)], ssem.at[35], rsem.at[37], partner
        ),
    ]

    @pl.when(last)
    def _():
        inner[0].start()

    send(tpl, ybuf, 2, 2, (ty, o))
    tell(1)
    loads[0].wait()
    loads[1].wait()
    for q in range(NQ):
        cspec[q, 0:STRIP, :] = jnp.dot(
            frame[0:STRIP, :], col[q], preferred_element_type=F32
        ).astype(BF)

    chosen = group[0]
    depth = jnp.float32(0.0)
    for g in range(4):
        depth = depth + jnp.where(chosen == g, defo[g], 0.0)
    depth = depth * jnp.float32(math.pi)
    k = lax.broadcasted_iota(jnp.int32, (KH, BLK), 0).astype(F32) / LROW
    angle = depth * (k * k) + 0.07
    ctf_s[...] = jnp.sin(angle)
    ctf_c[...] = jnp.cos(angle)

    arrive(ybuf, 2)
    fill = pltpu.make_async_copy(ybuf.at[c], tg.at[ty], lsem.at[6])
    fill.start()
    at = 3
    for dx in (1, 2, 3):
        xd = lax.rem(x + dx, 4)
        for core in (0, 1):
            for piece in (0, 1):
                src = tpl.at[core] if piece == 0 else ybuf.at[core]
                slot = t if piece == 0 else ty
                send(
                    src, tg.at[slot], at, 3 + (dx - 1) * 4 + c * 2 + piece,
                    (xd * 4 + yh * 2 + core, o),
                )
                at += 1
    send(tpl.at[other], tg.at[t], 15, 15, partner)
    send(ybuf.at[other], tg.at[ty], 16, 16, partner)

    told(1)
    tell(2)
    arrive(frame.at[pl.ds(STRIP, BLK)], 35)

    @pl.when(last)
    def _():
        inner[1].start()

    arrive(frame.at[pl.ds(STRIP + BLK, BLK)], 36)
    arrive(frame.at[pl.ds(2 * STRIP, BLK)], 37)
    keep1 = jnp.where(t < 15, 1.0, 0.0).astype(F32)
    keep2 = jnp.where(t < 14, 1.0, 0.0).astype(F32)
    row = lax.broadcasted_iota(jnp.int32, (TS, 2 * BLK), 0)
    keep = jnp.where(row < STRIP, keep1, keep2)
    for q in range(NQ):
        part = jnp.dot(frame[STRIP:LROW, :], col[q], preferred_element_type=F32)
        cspec[q, STRIP:LROW, :] = (part * keep).astype(BF)
    loads[2].wait()

    def spectrum(q):
        real, imag = combine(jnp.dot(rows[...], cspec[q], preferred_element_type=F32))
        spec[q, :, 0:BLK] = real
        spec[q, :, BLK:] = imag
        return real * real + imag * imag

    for i in range(2):
        psend[i] = spectrum(2 * other + i).astype(BF)
    send(psend, precv, 17, 17, partner)
    for i in range(2):
        pown[i, 0:KH, :] = spectrum(2 * c + i)
        pown[i, KH:KP, :] = jnp.zeros((KP - KH, BLK), F32)

    for dx in (1, 2, 3):
        xs = lax.rem(x + 4 - dx, 4)
        for core in (0, 1):
            for piece in (0, 1):
                row_of = yh if piece == 0 else 1 - yh
                arrive(tg.at[xs * 4 + row_of * 2 + core], 3 + (dx - 1) * 4 + core * 2 + piece)
    arrive(tg.at[j * 2 + other], 15)
    arrive(tg.at[x * 4 + (1 - yh) * 2 + other], 16)
    loads[5].wait()
    fill.wait()
    send(tg, tr, 18, 18, partner)

    told(2)
    tell(3)

    arrive(precv, 17)
    for i in range(2):
        pown[i, 0:KH, :] = pown[i, 0:KH, :] + precv[i].astype(F32)
        for n in range(CHIPS):
            comb[n, i] = pown[i, n * KC : (n + 1) * KC, :].astype(BF)
    for d in FAR_FIRST:
        to = lax.rem(j + d, CHIPS)
        send(comb.at[to], rsb.at[d - 1], 18 + d, 18 + d, near(to * 2 + c))

    arrive(tr, 18)
    for n, held in enumerate((tg, tr)):
        for s in range(16):
            tf[s * 24 : (s + 1) * 24, :] = held[s].astype(F32)
        values = tf[...]
        mean = jnp.sum(values) / (TS * TS)
        spread = jnp.sum(values * values) / (TS * TS) - mean * mean + 1e-05
        inverse = lax.rsqrt(jnp.full((1, 2 * BLK), spread, F32)) / (LROW * LCOL)
        rounded = values.astype(BF)
        for q in range(NQ):
            part = jnp.dot(rounded, col[q, 0:TS, :], preferred_element_type=F32)
            tspec[n, q] = ((part - mean * col_sum[q]) * inverse).astype(BF)

    for d in range(1, CHIPS):
        arrive(rsb.at[d - 1], 18 + d)
    total = comb[j].astype(F32)
    for d in range(1, CHIPS):
        total = total + rsb[d - 1].astype(F32)
    gall[c, j] = total.astype(BF)
    for d in FAR_FIRST:
        to = lax.rem(j + d, CHIPS)
        send(gall.at[c, j], gall.at[c, j], 25 + d, 25 + d, near(to * 2 + c))
    send(gall.at[c, j], gall.at[c, j], 38, 38, partner)
    told(3)
    tell(4)

    for n in range(2):
        for q in range(NQ):
            real, imag = combine(
                jnp.dot(rows[:, 0:TS], tspec[n, q], preferred_element_type=F32)
            )
            hsp[n, q, :, 0:BLK] = real
            hsp[n, q, :, BLK:] = imag

    for d in FAR_FIRST[::-1]:
        src = lax.rem(j + CHIPS - d, CHIPS)
        arrive(gall.at[c, src], 25 + d)
        send(gall.at[c, src], gall.at[c, src], 38 + d, 38 + d, partner)
    for d in range(CHIPS):
        arrive(gall.at[other, lax.rem(j + CHIPS - d, CHIPS)], 38 + d)

    def power(q):
        return jnp.concatenate([gall[q // 2, n, q % 2].astype(F32) for n in range(CHIPS)], 0)

    k = lax.broadcasted_iota(jnp.int32, (KP, BLK), 0)
    weight = jnp.where(k < LROW // 2, 2.0, 1.0) * jnp.where(k <= LROW // 2, 1.0, 0.0)
    weight = jnp.where(k == 0, 1.0, weight)
    summed = jnp.zeros((KP, BLK), F32)
    for q in range(NQ):
        summed = summed + power(q)
    average = jnp.sum(summed * weight) / (LROW * LCOL * 16.0)
    for q in range(NQ):
        lane = lax.broadcasted_iota(jnp.int32, (1, BLK), 1) + q * BLK
        lane = jnp.where(2 * lane < LCOL, lane, lane - LCOL).astype(F32) / LCOL
        phase = depth * (lane * lane)
        factor = -(ctf_s[...] * jnp.cos(phase) + ctf_c[...] * jnp.sin(phase))
        factor = factor * lax.rsqrt(power(q)[0:KH] / 16.0 + average)
        real, imag = spec[q, :, 0:BLK] * factor, spec[q, :, BLK:] * factor
        for n in range(2):
            h_re, h_im = hsp[n, q, :, 0:BLK], hsp[n, q, :, BLK:]
            qb[n * KH : (n + 1) * KH, q * 256 : q * 256 + BLK] = (real * h_re + imag * h_im).astype(BF)
            qb[n * KH : (n + 1) * KH, q * 256 + BLK : (q + 1) * 256] = (imag * h_re - real * h_im).astype(BF)
    loads[3].wait()
    loads[4].wait()
    for n in range(2):
        y = jnp.dot(
            qb[n * KH : (n + 1) * KH, :], back[...], preferred_element_type=F32
        ).astype(BF)
        ys[0:KH, n * BLK : (n + 1) * BLK] = y[:, 0:BLK]
        ys[KH:, n * BLK : (n + 1) * BLK] = y[:, BLK:]
    score = jnp.dot(outt[...], ys[...], preferred_element_type=F32)
    for n in range(32):
        block = score[n * 8 : (n + 1) * 8, :]
        sbuf[n] = jnp.concatenate([block[:, 0:BLK], block[:, BLK:]], 0).astype(BF)

    def a2a(d):
        to = lax.rem(o + d, 32)
        return remote(sbuf.at[to], rbuf.at[o], asem.at[d], bsem.at[d], (t, to))

    def a2a_start(i, carry):
        a2a(16 + (i + 1) // 2 * (1 - 2 * (i % 2))).start()
        return carry

    def a2a_wait(d, carry):
        src = lax.rem(o + 32 - d, 32)
        remote(rbuf.at[src], rbuf.at[src], asem.at[d], bsem.at[d], partner).wait_recv()
        return carry

    def a2a_sent(d, carry):
        a2a(d).wait_send()
        return carry

    told(4)
    lax.fori_loop(0, 31, a2a_start, 0)
    keep_own = pltpu.make_async_copy(sbuf.at[o], rbuf.at[o], lsem.at[7])
    keep_own.start()
    for copy in started:
        copy.wait_send()

    @pl.when(last)
    def _():
        for copy in inner:
            copy.wait_send()

    keep_own.wait()
    lax.fori_loop(1, 32, a2a_wait, 0)
    best = jnp.full((8, BLK), -jnp.inf, F32)
    first = jnp.zeros((8, BLK), F32)
    second = jnp.zeros((8, BLK), F32)
    for n in range(32):
        pair = rbuf[n].astype(F32)
        a, b = pair[0:8], pair[8:16]
        best = jnp.maximum(best, jnp.maximum(a, b))
        first = first + (a + b)
        second = second + (a * a + b * b)
    mean = first / 64.0
    spread = second / 64.0 - mean * mean
    res_o[0:8] = best
    res_o[8:16] = (best - mean) / jnp.sqrt(spread + 1e-05)
    lax.fori_loop(1, 32, a2a_sent, 0)


def local(consts, micrograph, templates, defocus, group_of_tile):
    rows, col, back, out, col_sum = consts
    hbm = pl.BlockSpec(memory_space=pl.ANY)
    vmem = pl.BlockSpec(memory_space=pltpu.VMEM)
    smem = pl.BlockSpec(memory_space=pltpu.SMEM)
    v = pltpu.VMEM
    both = pl.pallas_call(
        kernel,
        out_shape=jax.ShapeDtypeStruct((16, OUTC), F32),
        in_specs=[hbm, hbm, smem, smem, hbm, hbm, hbm, hbm, vmem],
        out_specs=vmem,
        scratch_shapes=[
            v((2 * KH, LROW), BF),
            v((NQ, LCOL, 2 * BLK), BF),
            v((2 * LCOL, 2 * OUTC), BF),
            v((STRIP, 2 * KH), BF),
            v((LROW, LCOL), BF),
            v((NQ, LROW, 2 * BLK), BF),
            v((NQ, KH, 2 * BLK), F32),
            v((2, 24, TS), BF),
            v((16, 24, TS), BF),
            v((16, 24, TS), BF),
            v((TS, TS), F32),
            v((2, NQ, TS, 2 * BLK), BF),
            v((2, NQ, KH, 2 * BLK), F32),
            v((2, KH, BLK), BF),
            v((2, KP, BLK), F32),
            v((2, KH, BLK), BF),
            v((CHIPS, 2, KC, BLK), BF),
            v((CHIPS - 1, 2, KC, BLK), BF),
            v((2, CHIPS, 2, KC, BLK), BF),
            v((KH, BLK), F32),
            v((KH, BLK), F32),
            v((2 * KH, 2 * LCOL), BF),
            v((2 * KH, 2 * BLK), BF),
            v((32, 16, BLK), BF),
            v((32, 16, BLK), BF),
            pltpu.SemaphoreType.DMA((8,)),
            pltpu.SemaphoreType.DMA((46,)),
            pltpu.SemaphoreType.DMA((46,)),
            pltpu.SemaphoreType.DMA((32,)),
            pltpu.SemaphoreType.DMA((32,)),
            pltpu.SemaphoreType.REGULAR((4,)),
        ],
        compiler_params=pltpu.CompilerParams(collective_id=0, has_side_effects=True),
        name="match",
    )(micrograph, templates, defocus, group_of_tile, rows, col, back, out, col_sum)
    return both[0:8], both[8:16]


def solution(mesh):
    consts = tuple(jnp.asarray(a) for a in tables())
    return jax.shard_map(
        functools.partial(local, consts),
        mesh=mesh,
        in_specs=(P("tile", None), P("orient", "tile", None), P(), P("tile")),
        out_specs=(P(("tile", "orient"), None),) * 2,
        check_vma=False,
    )
```

```python
import functools
import math

import jax
import jax.numpy as jnp
import numpy as np
from jax import lax
from jax.experimental import pallas as pl
from jax.experimental.pallas import tpu as pltpu
from jax.sharding import PartitionSpec as P

TS, STRIP, OUTC, LROW, LCOL = 384, 256, 128, 640, 512
KH = 336
KP = 384
BLK = 128
NQ = LCOL // BLK
CHIPS = 8
KC = KP // CHIPS
FAR_FIRST = (3, 5, 4, 2, 6, 1, 7)
MESH = pl.DeviceIdType.MESH
BF, F32 = jnp.bfloat16, jnp.float32


def twiddle(rows, cols, modulus, sign):
    residue = np.arange(rows)[:, None] * np.arange(cols)[None, :] % modulus
    mirrored = modulus - residue
    angle = np.minimum(residue, mirrored).astype(np.float32) * np.float32(2 * math.pi / modulus)
    flipped = np.where(residue > mirrored, -1.0, 1.0).astype(np.float32)
    return np.cos(angle).astype(BF), (np.float32(sign) * flipped * np.sin(angle)).astype(BF)


def tables():
    cc, cs = twiddle(LCOL, LCOL, LCOL, -1.0)
    col = np.stack(
        [
            np.concatenate([cc[:, q * BLK : (q + 1) * BLK], cs[:, q * BLK : (q + 1) * BLK]], 1)
            for q in range(NQ)
        ]
    )
    col_sum = col[:, :TS].astype(np.float32).sum(1, keepdims=True)
    rc, rs = twiddle(LROW, LROW, LROW, -1.0)
    rows = np.zeros((2 * KH, LROW), BF)
    half = LROW // 2 + 1
    rows[:half], rows[KH : KH + half] = rc[:half], rs[:half]
    bc, bs = twiddle(LCOL, OUTC, LCOL, 1.0)
    back = np.concatenate(
        [
            np.block(
                [
                    [bc[q * BLK : (q + 1) * BLK], bs[q * BLK : (q + 1) * BLK]],
                    [-bs[q * BLK : (q + 1) * BLK], bc[q * BLK : (q + 1) * BLK]],
                ]
            )
            for q in range(NQ)
        ]
    ).astype(BF)
    ac, as_ = twiddle(STRIP, LROW, LROW, 1.0)
    weight = np.full(half, 2.0, np.float32)
    weight[0] = weight[-1] = 1.0
    out = np.zeros((STRIP, 2 * KH), np.float32)
    out[:, :half] = weight * ac[:, :half].astype(np.float32)
    out[:, KH : KH + half] = -weight * as_[:, :half].astype(np.float32)
    return rows, col, back, out.astype(BF), col_sum


def combine(product, n=KH):
    real = product[:n, :BLK] - product[n:, BLK:]
    imag = product[:n, BLK:] + product[n:, :BLK]
    return real, imag


def kernel(
    mic, tpl, defo_h, group_h, rows_h, col_h, back_h, out_h, sum_h,
    res_o,
    rows, col, back, outt, defo, group, col_sum, frame, begun, spec, ybuf, tg, tr, tf, tspec, hsp,
    psend, precv, comb, rsb, gall, ctf_s, ctf_c, qb, ys, sbuf, rbuf,
    lsem, ssem, rsem, asem, bsem, esem,
):
    t, o = lax.axis_index("tile"), lax.axis_index("orient")
    z, ylo = o // 2, o % 2
    j, c = t // 2, t % 2
    x, yh = j // 2, j % 2
    other = 1 - c

    def orient_at(tile):
        return z * 2 + (ylo + yh + (tile // 2) % 2) % 2

    def near(tile):
        return (tile, orient_at(tile))

    loads = [
        pltpu.make_async_copy(mic, frame.at[pl.ds(0, STRIP)], lsem.at[0]),
        pltpu.make_async_copy(col_h, col, lsem.at[1]),
        pltpu.make_async_copy(rows_h, rows, lsem.at[2]),
        pltpu.make_async_copy(back_h, back, lsem.at[3]),
        pltpu.make_async_copy(out_h, outt, lsem.at[4]),
        pltpu.make_async_copy(tpl.at[c], tg.at[t], lsem.at[5]),
        pltpu.make_async_copy(defo_h, defo, lsem.at[9]),
        pltpu.make_async_copy(group_h, group, lsem.at[10]),
        pltpu.make_async_copy(sum_h, col_sum, lsem.at[11]),
    ]

    barrier = pltpu.get_barrier_semaphore()

    def greet(device):
        pl.semaphore_signal(barrier, inc=1, device_id=device, device_id_type=MESH)

    def orient_peer(d):
        return (t, lax.rem(o + d, 32))

    beside = near(lax.rem(j + CHIPS + 2 * c - 1, CHIPS) * 2 + other)
    greet(beside)
    for d in (1, 31):
        greet(orient_peer(d))
    ty = x * 4 + (1 - yh) * 2 + c
    greet((ty, o))
    partner = (j * 2 + other, o)
    greet(partner)
    for dx in (1, 2, 3):
        for core in (0, 1):
            greet((lax.rem(x + dx, 4) * 4 + yh * 2 + core, o))
    for d in range(1, CHIPS):
        greet(near(lax.rem(j + d, CHIPS) * 2 + c))

    for copy in loads:
        copy.start()
    started = []

    def remote(src, dst, send, recv, device):
        return pltpu.make_async_remote_copy(
            src_ref=src, dst_ref=dst, send_sem=send, recv_sem=recv, device_id=device, device_id_type=MESH
        )

    def send(src, dst, index, recv_index, device):
        copy = remote(src, dst, ssem.at[index], rsem.at[recv_index], device)
        copy.start()
        started.append(copy)

    def arrive(dst, index):
        remote(dst, dst, ssem.at[0], rsem.at[index], partner).wait_recv()

    def tell(r):
        step = max(1, 2 ** (r - 1))
        for d in (step, 32 - step):
            pl.semaphore_signal(
                esem.at[r - 1], inc=1, device_id=orient_peer(d), device_id_type=MESH
            )

    def told(r):
        pl.semaphore_wait(esem.at[r - 1], 2)

    pl.semaphore_wait(barrier, 1 + 2 + 1 + 1 + 6 + 7)

    before = lax.rem(j + CHIPS - 1, CHIPS)
    across = near(before * 2 + 1)
    last = c == 1
    first_rows, second_rows = mic.at[pl.ds(0, BLK)], mic.at[pl.ds(BLK, BLK)]
    send(
        first_rows, frame.at[pl.ds(pl.multiple_of(STRIP + STRIP * c, STRIP), BLK)],
        0, 35 + 2 * c, across,
    )
    there = (jnp.where(last, j, before) * 2 + other, jnp.where(last, o, across[1]))
    send(second_rows, frame.at[pl.ds(STRIP + BLK, BLK)], 1, 36, there)
    inner = [
        remote(first_rows, frame.at[pl.ds(STRIP, BLK)], ssem.at[34], rsem.at[35], partner),
        remote(
            frame.at[pl.ds(STRIP, BLK)], frame.at[pl.ds(2 * STRIP, BLK)], ssem.at[35], rsem.at[37], partner
        ),
    ]

    @pl.when(last)
    def _():
        inner[0].start()

    send(tpl, ybuf, 2, 2, (ty, o))
    tell(1)
    loads[0].wait()
    loads[1].wait()
    loads[2].wait()
    for q in range(NQ):
        part = jnp.dot(frame[0:STRIP, :], col[q], preferred_element_type=F32).astype(BF)
        begun[q] = jnp.dot(rows[:, 0:STRIP], part, preferred_element_type=F32)

    for n in (6, 7, 8):
        loads[n].wait()
    chosen = group[0]
    depth = jnp.float32(0.0)
    for g in range(4):
        depth = depth + jnp.where(chosen == g, defo[g], 0.0)
    depth = depth * jnp.float32(math.pi)
    k = lax.broadcasted_iota(jnp.int32, (KH, BLK), 0).astype(F32) / LROW
    angle = depth * (k * k) + 0.07
    ctf_s[...] = jnp.sin(angle)
    ctf_c[...] = jnp.cos(angle)

    arrive(ybuf, 2)
    fill = pltpu.make_async_copy(ybuf.at[c], tg.at[ty], lsem.at[6])
    fill.start()
    at = 3
    for dx in (1, 2, 3):
        xd = lax.rem(x + dx, 4)
        for core in (0, 1):
            for piece in (0, 1):
                src = tpl.at[core] if piece == 0 else ybuf.at[core]
                slot = t if piece == 0 else ty
                send(
                    src, tg.at[slot], at, 3 + (dx - 1) * 4 + c * 2 + piece,
                    (xd * 4 + yh * 2 + core, o),
                )
                at += 1
    send(tpl.at[other], tg.at[t], 15, 15, partner)
    send(ybuf.at[other], tg.at[ty], 16, 16, partner)

    told(1)
    tell(2)
    arrive(frame.at[pl.ds(STRIP, BLK)], 35)

    @pl.when(last)
    def _():
        inner[1].start()

    arrive(frame.at[pl.ds(STRIP + BLK, BLK)], 36)
    arrive(frame.at[pl.ds(2 * STRIP, BLK)], 37)
    keep1 = jnp.where(t < 15, 1.0, 0.0).astype(F32)
    keep2 = jnp.where(t < 14, 1.0, 0.0).astype(F32)
    row = lax.broadcasted_iota(jnp.int32, (TS, 2 * BLK), 0)
    keep = jnp.where(row < STRIP, keep1, keep2)

    def spectrum(q):
        part = jnp.dot(frame[STRIP:LROW, :], col[q], preferred_element_type=F32)
        part = (part * keep).astype(BF)
        real, imag = combine(
            begun[q] + jnp.dot(rows[:, STRIP:LROW], part, preferred_element_type=F32)
        )
        spec[q, :, 0:BLK] = real
        spec[q, :, BLK:] = imag
        return real * real + imag * imag

    for i in range(2):
        psend[i] = spectrum(2 * other + i).astype(BF)
        send(psend.at[i], precv.at[i], 17 + i, 17 + i, partner)

    for i in range(2):
        own = spectrum(2 * c + i)
        arrive(precv.at[i], 17 + i)
        own = own + precv[i].astype(F32)
        for n in range(CHIPS - 1):
            comb[i, n] = own[n * KC : (n + 1) * KC, :].astype(BF)
        comb[i, CHIPS - 1] = jnp.zeros((KC, BLK), BF)
        for d in FAR_FIRST:
            to = lax.rem(j + d, CHIPS)
            at = 39 + 7 * i + d
            send(comb.at[i, to], rsb.at[i, d - 1], at, at, near(to * 2 + c))
    told(2)
    tell(3)

    for dx in (1, 2, 3):
        xs = lax.rem(x + 4 - dx, 4)
        for core in (0, 1):
            for piece in (0, 1):
                row_of = yh if piece == 0 else 1 - yh
                arrive(tg.at[xs * 4 + row_of * 2 + core], 3 + (dx - 1) * 4 + core * 2 + piece)
    arrive(tg.at[j * 2 + other], 15)
    arrive(tg.at[x * 4 + (1 - yh) * 2 + other], 16)
    loads[5].wait()
    fill.wait()
    send(tg, tr, 19, 19, partner)

    for n, held in enumerate((tg, tr)):
        if n == 1:
            arrive(tr, 19)
        for s in range(16):
            tf[s * 24 : (s + 1) * 24, :] = held[s].astype(F32)
        values = tf[...]
        mean = jnp.sum(values) / (TS * TS)
        spread = jnp.sum(values * values) / (TS * TS) - mean * mean + 1e-05
        inverse = lax.rsqrt(jnp.full((1, 2 * BLK), spread, F32)) / (LROW * LCOL)
        rounded = values.astype(BF)
        for q in range(NQ):
            part = jnp.dot(rounded, col[q, 0:TS, :], preferred_element_type=F32)
            tspec[n, q] = ((part - mean * col_sum[q]) * inverse).astype(BF)

    for i in range(2):
        total = comb[i, j].astype(F32)
        for d in range(1, CHIPS):
            arrive(rsb.at[i, d - 1], 39 + 7 * i + d)
            total = total + rsb[i, d - 1].astype(F32)
        gall[c, i, j] = total.astype(BF)
        mine = gall.at[c, i, j]
        for d in FAR_FIRST:
            to = lax.rem(j + d, CHIPS)
            at = 53 + 7 * i + d
            send(mine, mine, at, at, near(to * 2 + c))
        send(mine, mine, 68 + 8 * i, 68 + 8 * i, partner)
    told(3)
    tell(4)

    for n in range(2):
        for q in range(NQ):
            real, imag = combine(
                jnp.dot(rows[:, 0:TS], tspec[n, q], preferred_element_type=F32)
            )
            hsp[n, q, :, 0:BLK] = real
            hsp[n, q, :, BLK:] = imag

    for i in range(2):
        for d in FAR_FIRST[::-1]:
            piece = gall.at[c, i, lax.rem(j + CHIPS - d, CHIPS)]
            arrive(piece, 53 + 7 * i + d)
            send(piece, piece, 68 + 8 * i + d, 68 + 8 * i + d, partner)
    for i in range(2):
        for d in range(CHIPS):
            arrive(gall.at[other, i, lax.rem(j + CHIPS - d, CHIPS)], 68 + 8 * i + d)

    def power(q):
        return jnp.concatenate([gall[q // 2, q % 2, n].astype(F32) for n in range(CHIPS)], 0)

    k = lax.broadcasted_iota(jnp.int32, (KP, BLK), 0)
    weight = jnp.where(k < LROW // 2, 2.0, 1.0) * jnp.where(k <= LROW // 2, 1.0, 0.0)
    weight = jnp.where(k == 0, 1.0, weight)
    summed = jnp.zeros((KP, BLK), F32)
    for q in range(NQ):
        summed = summed + power(q)
    average = jnp.sum(summed * weight) / (LROW * LCOL * 16.0)
    for q in range(NQ):
        lane = lax.broadcasted_iota(jnp.int32, (1, BLK), 1) + q * BLK
        lane = jnp.where(2 * lane < LCOL, lane, lane - LCOL).astype(F32) / LCOL
        phase = depth * (lane * lane)
        factor = -(ctf_s[...] * jnp.cos(phase) + ctf_c[...] * jnp.sin(phase))
        factor = factor * lax.rsqrt(power(q)[0:KH] / 16.0 + average)
        spec[q, :, 0:BLK] = spec[q, :, 0:BLK] * factor
        spec[q, :, BLK:] = spec[q, :, BLK:] * factor
    loads[3].wait()
    loads[4].wait()
    told(4)

    def a2a(d):
        to = lax.rem(o + d, 32)
        return remote(sbuf.at[to], rbuf.at[o], asem.at[d], bsem.at[d], (t, to))

    for n in range(2):
        for q in range(NQ):
            real, imag = spec[q, :, 0:BLK], spec[q, :, BLK:]
            h_re, h_im = hsp[n, q, :, 0:BLK], hsp[n, q, :, BLK:]
            qb[n, :, q * 256 : q * 256 + BLK] = (real * h_re + imag * h_im).astype(BF)
            qb[n, :, q * 256 + BLK : (q + 1) * 256] = (imag * h_re - real * h_im).astype(BF)
        y = jnp.dot(qb[n], back[...], preferred_element_type=F32).astype(BF)
        ys[0:KH, n * BLK : (n + 1) * BLK] = y[:, 0:BLK]
        ys[KH:, n * BLK : (n + 1) * BLK] = y[:, BLK:]
    score = jnp.dot(outt[...], ys[...], preferred_element_type=F32)
    for r in range(32):
        block = score[r * 8 : (r + 1) * 8, :]
        sbuf[r] = jnp.concatenate([block[:, 0:BLK], block[:, BLK:]], 0).astype(BF)

    def a2a_start(i, carry):
        a2a(16 + (i + 1) // 2 * (1 - 2 * (i % 2))).start()
        return carry

    lax.fori_loop(0, 31, a2a_start, 0)
    own_rows = pltpu.make_async_copy(sbuf.at[o], rbuf.at[o], lsem.at[7])
    own_rows.start()

    def a2a_wait(d, carry):
        src = lax.rem(o + 32 - d, 32)
        remote(rbuf.at[src], rbuf.at[src], asem.at[d], bsem.at[d], partner).wait_recv()
        return carry

    def a2a_sent(d, carry):
        a2a(d).wait_send()
        return carry

    for copy in started:
        copy.wait_send()

    @pl.when(last)
    def _():
        for copy in inner:
            copy.wait_send()

    own_rows.wait()
    lax.fori_loop(1, 32, a2a_wait, 0)
    best = jnp.full((8, BLK), -jnp.inf, F32)
    first = jnp.zeros((8, BLK), F32)
    second = jnp.zeros((8, BLK), F32)
    for r in range(32):
        pair = rbuf[r].astype(F32)
        a, b = pair[0:8], pair[8:16]
        best = jnp.maximum(best, jnp.maximum(a, b))
        first = first + (a + b)
        second = second + (a * a + b * b)
    mean = first / 64.0
    spread = second / 64.0 - mean * mean
    res_o[0:8] = best
    res_o[8:16] = (best - mean) / jnp.sqrt(spread + 1e-05)
    lax.fori_loop(1, 32, a2a_sent, 0)


def local(consts, micrograph, templates, defocus, group_of_tile):
    rows, col, back, out, col_sum = consts
    hbm = pl.BlockSpec(memory_space=pltpu.HBM)
    vmem = pl.BlockSpec(memory_space=pltpu.VMEM)
    v = pltpu.VMEM
    both = pl.pallas_call(
        kernel,
        out_shape=pltpu.VMEM((16, OUTC), F32),
        in_specs=[hbm] * 9,
        out_specs=vmem,
        scratch_shapes=[
            v((2 * KH, LROW), BF),
            v((NQ, LCOL, 2 * BLK), BF),
            v((2 * LCOL, 2 * OUTC), BF),
            v((STRIP, 2 * KH), BF),
            pltpu.SMEM((4,), F32),
            pltpu.SMEM((1,), jnp.int32),
            v((NQ, 1, 2 * BLK), F32),
            v((LROW, LCOL), BF),
            v((NQ, 2 * KH, 2 * BLK), F32),
            v((NQ, KH, 2 * BLK), F32),
            v((2, 24, TS), BF),
            v((16, 24, TS), BF),
            v((16, 24, TS), BF),
            v((TS, TS), F32),
            v((2, NQ, TS, 2 * BLK), BF),
            v((2, NQ, KH, 2 * BLK), F32),
            v((2, KH, BLK), BF),
            v((2, KH, BLK), BF),
            v((2, CHIPS, KC, BLK), BF),
            v((2, CHIPS - 1, KC, BLK), BF),
            v((2, 2, CHIPS, KC, BLK), BF),
            v((KH, BLK), F32),
            v((KH, BLK), F32),
            v((2, KH, 2 * LCOL), BF),
            v((2 * KH, 2 * BLK), BF),
            v((32, 16, BLK), BF),
            v((32, 16, BLK), BF),
            pltpu.SemaphoreType.DMA((12,)),
            pltpu.SemaphoreType.DMA((84,)),
            pltpu.SemaphoreType.DMA((84,)),
            pltpu.SemaphoreType.DMA((32,)),
            pltpu.SemaphoreType.DMA((32,)),
            pltpu.SemaphoreType.REGULAR((4,)),
        ],
        compiler_params=pltpu.CompilerParams(collective_id=0, has_side_effects=True),
        name="match",
    )(micrograph, templates, defocus, group_of_tile, rows, col, back, out, col_sum)
    return both[0:8], both[8:16]


def solution(mesh):
    consts = tuple(jnp.asarray(a) for a in tables())
    return jax.shard_map(
        functools.partial(local, consts),
        mesh=mesh,
        in_specs=(P("tile", None), P("orient", "tile", None), P(), P("tile")),
        out_specs=(P(("tile", "orient"), None),) * 2,
        check_vma=False,
    )
```

```python
import functools
import math

import jax
import jax.numpy as jnp
import numpy as np
from jax import lax
from jax.experimental import pallas as pl
from jax.experimental.pallas import tpu as pltpu
from jax.sharding import PartitionSpec as P

TS, STRIP, OUTC, LROW, LCOL = 384, 256, 128, 640, 512
KH = 336
KP = 384
BLK = 128
NQ = LCOL // BLK
CHIPS = 8
KC = KP // CHIPS
FAR_FIRST = (3, 5, 4, 2, 6, 1, 7)
MESH = pl.DeviceIdType.MESH
BF, F32 = jnp.bfloat16, jnp.float32


def twiddle(rows, cols, modulus, sign):
    residue = np.arange(rows)[:, None] * np.arange(cols)[None, :] % modulus
    mirrored = modulus - residue
    angle = np.minimum(residue, mirrored).astype(np.float32) * np.float32(2 * math.pi / modulus)
    flipped = np.where(residue > mirrored, -1.0, 1.0).astype(np.float32)
    return np.cos(angle).astype(BF), (np.float32(sign) * flipped * np.sin(angle)).astype(BF)


def tables():
    cc, cs = twiddle(LCOL, LCOL, LCOL, -1.0)
    col = np.stack(
        [
            np.concatenate([cc[:, q * BLK : (q + 1) * BLK], cs[:, q * BLK : (q + 1) * BLK]], 1)
            for q in range(NQ)
        ]
    )
    col_sum = col[:, :TS].astype(np.float32).sum(1, keepdims=True)
    rc, rs = twiddle(LROW, LROW, LROW, -1.0)
    rows = np.zeros((2 * KH, LROW), BF)
    half = LROW // 2 + 1
    rows[:half], rows[KH : KH + half] = rc[:half], rs[:half]
    bc, bs = twiddle(LCOL, OUTC, LCOL, 1.0)
    back = np.concatenate(
        [
            np.block(
                [
                    [bc[q * BLK : (q + 1) * BLK], bs[q * BLK : (q + 1) * BLK]],
                    [-bs[q * BLK : (q + 1) * BLK], bc[q * BLK : (q + 1) * BLK]],
                ]
            )
            for q in range(NQ)
        ]
    ).astype(BF)
    ac, as_ = twiddle(STRIP, LROW, LROW, 1.0)
    weight = np.full(half, 2.0, np.float32)
    weight[0] = weight[-1] = 1.0
    out = np.zeros((STRIP, 2 * KH), np.float32)
    out[:, :half] = weight * ac[:, :half].astype(np.float32)
    out[:, KH : KH + half] = -weight * as_[:, :half].astype(np.float32)
    return rows, col, back, out.astype(BF), col_sum


def combine(product, n=KH):
    real = product[:n, :BLK] - product[n:, BLK:]
    imag = product[:n, BLK:] + product[n:, :BLK]
    return real, imag


def kernel(
    mic, tpl, defo_h, group_h, rows_h, col_h, back_h, out_h, sum_h,
    res_o,
    rows, col, back, outt, defo, group, col_sum, frame, begun, spec, ybuf, tg, tr, tf, tspec, hsp,
    psend, precv, comb, rsb, gall, ctf_s, ctf_c, qb, ys, sbuf, rbuf,
    lsem, ssem, rsem, asem, bsem, esem,
):
    t, o = lax.axis_index("tile"), lax.axis_index("orient")
    z, ylo = o // 2, o % 2
    j, c = t // 2, t % 2
    x, yh = j // 2, j % 2
    other = 1 - c

    def orient_at(tile):
        return z * 2 + (ylo + yh + (tile // 2) % 2) % 2

    def near(tile):
        return (tile, orient_at(tile))

    loads = [
        pltpu.make_async_copy(mic, frame.at[pl.ds(0, STRIP)], lsem.at[0]),
        pltpu.make_async_copy(col_h, col, lsem.at[1]),
        pltpu.make_async_copy(rows_h, rows, lsem.at[2]),
        pltpu.make_async_copy(back_h, back, lsem.at[3]),
        pltpu.make_async_copy(out_h, outt, lsem.at[4]),
        pltpu.make_async_copy(tpl.at[c], tg.at[t], lsem.at[5]),
        pltpu.make_async_copy(defo_h, defo, lsem.at[9]),
        pltpu.make_async_copy(group_h, group, lsem.at[10]),
        pltpu.make_async_copy(sum_h, col_sum, lsem.at[11]),
    ]

    barrier = pltpu.get_barrier_semaphore()

    def greet(device):
        pl.semaphore_signal(barrier, inc=1, device_id=device, device_id_type=MESH)

    def orient_peer(d):
        return (t, lax.rem(o + d, 32))

    beside = near(lax.rem(j + CHIPS + 2 * c - 1, CHIPS) * 2 + other)
    greet(beside)
    for d in (1, 31):
        greet(orient_peer(d))
    ty = x * 4 + (1 - yh) * 2 + c
    greet((ty, o))
    partner = (j * 2 + other, o)
    greet(partner)
    for dx in (1, 2, 3):
        for core in (0, 1):
            greet((lax.rem(x + dx, 4) * 4 + yh * 2 + core, o))
    for d in range(1, CHIPS):
        greet(near(lax.rem(j + d, CHIPS) * 2 + c))

    for copy in loads:
        copy.start()
    started = []

    def remote(src, dst, send, recv, device):
        return pltpu.make_async_remote_copy(
            src_ref=src, dst_ref=dst, send_sem=send, recv_sem=recv, device_id=device, device_id_type=MESH
        )

    def send(src, dst, index, recv_index, device):
        copy = remote(src, dst, ssem.at[index], rsem.at[recv_index], device)
        copy.start()
        started.append(copy)

    def arrive(dst, index):
        remote(dst, dst, ssem.at[0], rsem.at[index], partner).wait_recv()

    def tell(r):
        step = max(1, 2 ** (r - 1))
        for d in (step, 32 - step):
            pl.semaphore_signal(
                esem.at[r - 1], inc=1, device_id=orient_peer(d), device_id_type=MESH
            )

    def told(r):
        pl.semaphore_wait(esem.at[r - 1], 2)

    pl.semaphore_wait(barrier, 1 + 2 + 1 + 1 + 6 + 7)

    before = lax.rem(j + CHIPS - 1, CHIPS)
    across = near(before * 2 + 1)
    last = c == 1
    first_rows, second_rows = mic.at[pl.ds(0, BLK)], mic.at[pl.ds(BLK, BLK)]
    send(
        first_rows, frame.at[pl.ds(pl.multiple_of(STRIP + STRIP * c, STRIP), BLK)],
        0, 35 + 2 * c, across,
    )
    there = (jnp.where(last, j, before) * 2 + other, jnp.where(last, o, across[1]))
    send(second_rows, frame.at[pl.ds(STRIP + BLK, BLK)], 1, 36, there)
    inner = [
        remote(first_rows, frame.at[pl.ds(STRIP, BLK)], ssem.at[34], rsem.at[35], partner),
        remote(
            frame.at[pl.ds(STRIP, BLK)], frame.at[pl.ds(2 * STRIP, BLK)], ssem.at[35], rsem.at[37], partner
        ),
    ]

    @pl.when(last)
    def _():
        inner[0].start()

    send(tpl, ybuf, 2, 2, (ty, o))
    tell(1)
    loads[0].wait()
    loads[1].wait()
    loads[2].wait()
    for q in range(NQ):
        part = jnp.dot(frame[0:STRIP, :], col[q], preferred_element_type=F32).astype(BF)
        begun[q] = jnp.dot(rows[:, 0:STRIP], part, preferred_element_type=F32)

    for n in (6, 7, 8):
        loads[n].wait()
    chosen = group[0]
    depth = jnp.float32(0.0)
    for g in range(4):
        depth = depth + jnp.where(chosen == g, defo[g], 0.0)
    depth = depth * jnp.float32(math.pi)
    k = lax.broadcasted_iota(jnp.int32, (KH, BLK), 0).astype(F32) / LROW
    angle = depth * (k * k) + 0.07
    ctf_s[...] = jnp.sin(angle)
    ctf_c[...] = jnp.cos(angle)

    arrive(ybuf, 2)
    fill = pltpu.make_async_copy(ybuf.at[c], tg.at[ty], lsem.at[6])
    fill.start()
    at = 3
    for dx in (1, 2, 3):
        xd = lax.rem(x + dx, 4)
        for core in (0, 1):
            for piece in (0, 1):
                src = tpl.at[core] if piece == 0 else ybuf.at[core]
                slot = t if piece == 0 else ty
                send(
                    src, tg.at[slot], at, 3 + (dx - 1) * 4 + c * 2 + piece,
                    (xd * 4 + yh * 2 + core, o),
                )
                at += 1
    send(tpl.at[other], tg.at[t], 15, 15, partner)
    send(ybuf.at[other], tg.at[ty], 16, 16, partner)

    told(1)
    tell(2)
    arrive(frame.at[pl.ds(STRIP, BLK)], 35)

    @pl.when(last)
    def _():
        inner[1].start()

    arrive(frame.at[pl.ds(STRIP + BLK, BLK)], 36)
    arrive(frame.at[pl.ds(2 * STRIP, BLK)], 37)
    keep1 = jnp.where(t < 15, 1.0, 0.0).astype(F32)
    keep2 = jnp.where(t < 14, 1.0, 0.0).astype(F32)
    row = lax.broadcasted_iota(jnp.int32, (TS, 2 * BLK), 0)
    keep = jnp.where(row < STRIP, keep1, keep2)

    def spectrum(q):
        part = jnp.dot(frame[STRIP:LROW, :], col[q], preferred_element_type=F32)
        part = (part * keep).astype(BF)
        real, imag = combine(
            begun[q] + jnp.dot(rows[:, STRIP:LROW], part, preferred_element_type=F32)
        )
        spec[q, :, 0:BLK] = real
        spec[q, :, BLK:] = imag
        return real * real + imag * imag

    for i in range(2):
        psend[i] = spectrum(2 * other + i).astype(BF)
        send(psend.at[i], precv.at[i], 17 + i, 17 + i, partner)

    for i in range(2):
        own = spectrum(2 * c + i)
        arrive(precv.at[i], 17 + i)
        own = own + precv[i].astype(F32)
        for n in range(CHIPS - 1):
            comb[i, n] = own[n * KC : (n + 1) * KC, :].astype(BF)
        comb[i, CHIPS - 1] = jnp.zeros((KC, BLK), BF)
        for d in FAR_FIRST:
            to = lax.rem(j + d, CHIPS)
            at = 39 + 7 * i + d
            send(comb.at[i, to], rsb.at[i, d - 1], at, at, near(to * 2 + c))
    told(2)
    tell(3)

    for dx in (1, 2, 3):
        xs = lax.rem(x + 4 - dx, 4)
        for core in (0, 1):
            for piece in (0, 1):
                row_of = yh if piece == 0 else 1 - yh
                arrive(tg.at[xs * 4 + row_of * 2 + core], 3 + (dx - 1) * 4 + core * 2 + piece)
    arrive(tg.at[j * 2 + other], 15)
    arrive(tg.at[x * 4 + (1 - yh) * 2 + other], 16)
    loads[5].wait()
    fill.wait()
    send(tg, tr, 19, 19, partner)

    for n, held in enumerate((tg, tr)):
        if n == 1:
            arrive(tr, 19)
        for s in range(16):
            tf[s * 24 : (s + 1) * 24, :] = held[s].astype(F32)
        values = tf[...]
        mean = jnp.sum(values) / (TS * TS)
        spread = jnp.sum(values * values) / (TS * TS) - mean * mean + 1e-05
        inverse = lax.rsqrt(jnp.full((1, 2 * BLK), spread, F32)) / (LROW * LCOL)
        rounded = values.astype(BF)
        for q in range(NQ):
            part = jnp.dot(rounded, col[q, 0:TS, :], preferred_element_type=F32)
            tspec[n, q] = ((part - mean * col_sum[q]) * inverse).astype(BF)

    for i in range(2):
        total = comb[i, j].astype(F32)
        for d in range(1, CHIPS):
            arrive(rsb.at[i, d - 1], 39 + 7 * i + d)
            total = total + rsb[i, d - 1].astype(F32)
        gall[c, i, j] = total.astype(BF)
        mine = gall.at[c, i, j]
        for d in FAR_FIRST:
            to = lax.rem(j + d, CHIPS)
            at = 53 + 7 * i + d
            send(mine, mine, at, at, near(to * 2 + c))
        send(mine, mine, 68 + 8 * i, 68 + 8 * i, partner)
    told(3)
    tell(4)

    for n in range(2):
        for q in range(NQ):
            real, imag = combine(
                jnp.dot(rows[:, 0:TS], tspec[n, q], preferred_element_type=F32)
            )
            hsp[n, q, :, 0:BLK] = real
            hsp[n, q, :, BLK:] = imag

    for i in range(2):
        for d in FAR_FIRST[::-1]:
            piece = gall.at[c, i, lax.rem(j + CHIPS - d, CHIPS)]
            arrive(piece, 53 + 7 * i + d)
            send(piece, piece, 68 + 8 * i + d, 68 + 8 * i + d, partner)
    for i in range(2):
        for d in range(CHIPS):
            arrive(gall.at[other, i, lax.rem(j + CHIPS - d, CHIPS)], 68 + 8 * i + d)

    def power(q):
        return jnp.concatenate([gall[q // 2, q % 2, n].astype(F32) for n in range(CHIPS)], 0)

    k = lax.broadcasted_iota(jnp.int32, (KP, BLK), 0)
    weight = jnp.where(k < LROW // 2, 2.0, 1.0) * jnp.where(k <= LROW // 2, 1.0, 0.0)
    weight = jnp.where(k == 0, 1.0, weight)
    summed = jnp.zeros((KP, BLK), F32)
    for q in range(NQ):
        summed = summed + power(q)
    average = jnp.sum(summed * weight) / (LROW * LCOL * 16.0)
    for q in range(NQ):
        lane = lax.broadcasted_iota(jnp.int32, (1, BLK), 1) + q * BLK
        lane = jnp.where(2 * lane < LCOL, lane, lane - LCOL).astype(F32) / LCOL
        phase = depth * (lane * lane)
        factor = -(ctf_s[...] * jnp.cos(phase) + ctf_c[...] * jnp.sin(phase))
        factor = factor * lax.rsqrt(power(q)[0:KH] / 16.0 + average)
        spec[q, :, 0:BLK] = spec[q, :, 0:BLK] * factor
        spec[q, :, BLK:] = spec[q, :, BLK:] * factor
    loads[3].wait()
    loads[4].wait()
    told(4)

    def a2a(d):
        to = lax.rem(o + d, 32)
        return remote(sbuf.at[to], rbuf.at[o], asem.at[d], bsem.at[d], (t, to))

    for n in range(2):
        for q in range(NQ):
            real, imag = spec[q, :, 0:BLK], spec[q, :, BLK:]
            h_re, h_im = hsp[n, q, :, 0:BLK], hsp[n, q, :, BLK:]
            qb[n, :, q * 256 : q * 256 + BLK] = (real * h_re + imag * h_im).astype(BF)
            qb[n, :, q * 256 + BLK : (q + 1) * 256] = (imag * h_re - real * h_im).astype(BF)
        y = jnp.dot(qb[n], back[...], preferred_element_type=F32).astype(BF)
        ys[0:KH, n * BLK : (n + 1) * BLK] = y[:, 0:BLK]
        ys[KH:, n * BLK : (n + 1) * BLK] = y[:, BLK:]
    score = jnp.dot(outt[...], ys[...], preferred_element_type=F32)
    for r in range(32):
        block = score[r * 8 : (r + 1) * 8, :]
        sbuf[r] = jnp.concatenate([block[:, 0:BLK], block[:, BLK:]], 0).astype(BF)

    for i in range(31):
        a2a(16 + (i + 1) // 2 * (1 - 2 * (i % 2))).start()
    own_rows = pltpu.make_async_copy(sbuf.at[o], rbuf.at[o], lsem.at[7])
    own_rows.start()

    def a2a_wait(d):
        src = lax.rem(o + 32 - d, 32)
        remote(rbuf.at[src], rbuf.at[src], asem.at[d], bsem.at[d], partner).wait_recv()

    for copy in started:
        copy.wait_send()

    @pl.when(last)
    def _():
        for copy in inner:
            copy.wait_send()

    own_rows.wait()
    for d in range(1, 32):
        a2a_wait(d)
    best = jnp.full((8, BLK), -jnp.inf, F32)
    first = jnp.zeros((8, BLK), F32)
    second = jnp.zeros((8, BLK), F32)
    for r in range(32):
        pair = rbuf[r].astype(F32)
        a, b = pair[0:8], pair[8:16]
        best = jnp.maximum(best, jnp.maximum(a, b))
        first = first + (a + b)
        second = second + (a * a + b * b)
    mean = first / 64.0
    spread = second / 64.0 - mean * mean
    res_o[0:8] = best
    res_o[8:16] = (best - mean) / jnp.sqrt(spread + 1e-05)
    for d in range(1, 32):
        a2a(d).wait_send()


def local(consts, micrograph, templates, defocus, group_of_tile):
    rows, col, back, out, col_sum = consts
    hbm = pl.BlockSpec(memory_space=pltpu.HBM)
    vmem = pl.BlockSpec(memory_space=pltpu.VMEM)
    v = pltpu.VMEM
    both = pl.pallas_call(
        kernel,
        out_shape=pltpu.VMEM((16, OUTC), F32),
        in_specs=[hbm] * 9,
        out_specs=vmem,
        scratch_shapes=[
            v((2 * KH, LROW), BF),
            v((NQ, LCOL, 2 * BLK), BF),
            v((2 * LCOL, 2 * OUTC), BF),
            v((STRIP, 2 * KH), BF),
            pltpu.SMEM((4,), F32),
            pltpu.SMEM((1,), jnp.int32),
            v((NQ, 1, 2 * BLK), F32),
            v((LROW, LCOL), BF),
            v((NQ, 2 * KH, 2 * BLK), F32),
            v((NQ, KH, 2 * BLK), F32),
            v((2, 24, TS), BF),
            v((16, 24, TS), BF),
            v((16, 24, TS), BF),
            v((TS, TS), F32),
            v((2, NQ, TS, 2 * BLK), BF),
            v((2, NQ, KH, 2 * BLK), F32),
            v((2, KH, BLK), BF),
            v((2, KH, BLK), BF),
            v((2, CHIPS, KC, BLK), BF),
            v((2, CHIPS - 1, KC, BLK), BF),
            v((2, 2, CHIPS, KC, BLK), BF),
            v((KH, BLK), F32),
            v((KH, BLK), F32),
            v((2, KH, 2 * LCOL), BF),
            v((2 * KH, 2 * BLK), BF),
            v((32, 16, BLK), BF),
            v((32, 16, BLK), BF),
            pltpu.SemaphoreType.DMA((12,)),
            pltpu.SemaphoreType.DMA((84,)),
            pltpu.SemaphoreType.DMA((84,)),
            pltpu.SemaphoreType.DMA((32,)),
            pltpu.SemaphoreType.DMA((32,)),
            pltpu.SemaphoreType.REGULAR((4,)),
        ],
        compiler_params=pltpu.CompilerParams(collective_id=0, has_side_effects=True),
        name="match",
    )(micrograph, templates, defocus, group_of_tile, rows, col, back, out, col_sum)
    return both[0:8], both[8:16]


def solution(mesh):
    consts = tuple(jnp.asarray(a) for a in tables())
    return jax.shard_map(
        functools.partial(local, consts),
        mesh=mesh,
        in_specs=(P("tile", None), P("orient", "tile", None), P(), P("tile")),
        out_specs=(P(("tile", "orient"), None),) * 2,
        check_vma=False,
    )
```

```python
import functools
import math

import jax
import jax.numpy as jnp
import numpy as np
from jax import lax
from jax.experimental import pallas as pl
from jax.experimental.pallas import tpu as pltpu
from jax.sharding import PartitionSpec as P

TS, STRIP, OUTC, LROW, LCOL = 384, 256, 128, 640, 512
KH = 336
KP = 384
BLK = 128
NQ = LCOL // BLK
CHIPS = 8
KC = KP // CHIPS
FAR_FIRST = (3, 5, 4, 2, 6, 1, 7)
MESH = pl.DeviceIdType.MESH
BF, F32 = jnp.bfloat16, jnp.float32


def twiddle(rows, cols, modulus, sign):
    residue = np.arange(rows)[:, None] * np.arange(cols)[None, :] % modulus
    mirrored = modulus - residue
    angle = np.minimum(residue, mirrored).astype(np.float32) * np.float32(2 * math.pi / modulus)
    flipped = np.where(residue > mirrored, -1.0, 1.0).astype(np.float32)
    return np.cos(angle).astype(BF), (np.float32(sign) * flipped * np.sin(angle)).astype(BF)


def tables():
    cc, cs = twiddle(LCOL, LCOL, LCOL, -1.0)
    col = np.stack(
        [
            np.concatenate([cc[:, q * BLK : (q + 1) * BLK], cs[:, q * BLK : (q + 1) * BLK]], 1)
            for q in range(NQ)
        ]
    )
    col_sum = col[:, :TS].astype(np.float32).sum(1, keepdims=True)
    rc, rs = twiddle(LROW, LROW, LROW, -1.0)
    rows = np.zeros((2 * KH, LROW), BF)
    half = LROW // 2 + 1
    rows[:half], rows[KH : KH + half] = rc[:half], rs[:half]
    bc, bs = twiddle(LCOL, OUTC, LCOL, 1.0)
    back = np.concatenate(
        [
            np.block(
                [
                    [bc[q * BLK : (q + 1) * BLK], bs[q * BLK : (q + 1) * BLK]],
                    [-bs[q * BLK : (q + 1) * BLK], bc[q * BLK : (q + 1) * BLK]],
                ]
            )
            for q in range(NQ)
        ]
    ).astype(BF)
    ac, as_ = twiddle(STRIP, LROW, LROW, 1.0)
    weight = np.full(half, 2.0, np.float32)
    weight[0] = weight[-1] = 1.0
    out = np.zeros((STRIP, 2 * KH), np.float32)
    out[:, :half] = weight * ac[:, :half].astype(np.float32)
    out[:, KH : KH + half] = -weight * as_[:, :half].astype(np.float32)
    return rows, col, back, out.astype(BF), col_sum


def combine(product, n=KH):
    real = product[:n, :BLK] - product[n:, BLK:]
    imag = product[:n, BLK:] + product[n:, :BLK]
    return real, imag


def kernel(
    mic, tpl, defo_h, group_h, rows_h, col_h, back_h, out_h, sum_h,
    res_o,
    rows, col, back, outt, defo, group, col_sum, frame, begun, spec, ybuf, tg, tr, tf, tspec, hsp,
    psend, precv, comb, rsb, gall, ctf_s, ctf_c, qb, ys, sbuf, rbuf,
    lsem, ssem, rsem, asem, bsem, esem,
):
    t, o = lax.axis_index("tile"), lax.axis_index("orient")
    z, ylo = o // 2, o % 2
    j, c = t // 2, t % 2
    x, yh = j // 2, j % 2
    other = 1 - c

    def orient_at(tile):
        return z * 2 + (ylo + yh + (tile // 2) % 2) % 2

    def near(tile):
        return (tile, orient_at(tile))

    loads = [
        pltpu.make_async_copy(mic, frame.at[pl.ds(0, STRIP)], lsem.at[0]),
        pltpu.make_async_copy(col_h, col, lsem.at[1]),
        pltpu.make_async_copy(rows_h, rows, lsem.at[2]),
        pltpu.make_async_copy(back_h, back, lsem.at[3]),
        pltpu.make_async_copy(out_h, outt, lsem.at[4]),
        pltpu.make_async_copy(tpl.at[c], tg.at[t], lsem.at[5]),
        pltpu.make_async_copy(defo_h, defo, lsem.at[9]),
        pltpu.make_async_copy(group_h, group, lsem.at[10]),
        pltpu.make_async_copy(sum_h, col_sum, lsem.at[11]),
    ]

    barrier = pltpu.get_barrier_semaphore()

    def greet(device):
        pl.semaphore_signal(barrier, inc=1, device_id=device, device_id_type=MESH)

    def orient_peer(d):
        return (t, lax.rem(o + d, 32))

    beside = near(lax.rem(j + CHIPS + 2 * c - 1, CHIPS) * 2 + other)
    greet(beside)
    for d in (1, 31):
        greet(orient_peer(d))
    ty = x * 4 + (1 - yh) * 2 + c
    greet((ty, o))
    partner = (j * 2 + other, o)
    greet(partner)
    for dx in (1, 2, 3):
        for core in (0, 1):
            greet((lax.rem(x + dx, 4) * 4 + yh * 2 + core, o))
    for d in range(1, CHIPS):
        greet(near(lax.rem(j + d, CHIPS) * 2 + c))

    for copy in loads:
        copy.start()
    started = []

    def remote(src, dst, send, recv, device):
        return pltpu.make_async_remote_copy(
            src_ref=src, dst_ref=dst, send_sem=send, recv_sem=recv, device_id=device, device_id_type=MESH
        )

    def send(src, dst, index, recv_index, device):
        copy = remote(src, dst, ssem.at[index], rsem.at[recv_index], device)
        copy.start()
        started.append(copy)

    def arrive(dst, index):
        remote(dst, dst, ssem.at[0], rsem.at[index], partner).wait_recv()

    def tell(r):
        step = max(1, 2 ** (r - 1))
        for d in (step, 32 - step):
            pl.semaphore_signal(
                esem.at[r - 1], inc=1, device_id=orient_peer(d), device_id_type=MESH
            )

    def told(r):
        pl.semaphore_wait(esem.at[r - 1], 2)

    pl.semaphore_wait(barrier, 1 + 2 + 1 + 1 + 6 + 7)

    before = lax.rem(j + CHIPS - 1, CHIPS)
    across = near(before * 2 + 1)
    last = c == 1
    first_rows, second_rows = mic.at[pl.ds(0, BLK)], mic.at[pl.ds(BLK, BLK)]
    send(
        first_rows, frame.at[pl.ds(pl.multiple_of(STRIP + STRIP * c, STRIP), BLK)],
        0, 35 + 2 * c, across,
    )
    there = (jnp.where(last, j, before) * 2 + other, jnp.where(last, o, across[1]))
    send(second_rows, frame.at[pl.ds(STRIP + BLK, BLK)], 1, 36, there)
    inner = [
        remote(first_rows, frame.at[pl.ds(STRIP, BLK)], ssem.at[34], rsem.at[35], partner),
        remote(
            frame.at[pl.ds(STRIP, BLK)], frame.at[pl.ds(2 * STRIP, BLK)], ssem.at[35], rsem.at[37], partner
        ),
    ]

    @pl.when(last)
    def _():
        inner[0].start()

    send(tpl, ybuf, 2, 2, (ty, o))
    tell(1)
    loads[0].wait()
    loads[1].wait()
    loads[2].wait()
    for q in range(NQ):
        part = jnp.dot(frame[0:STRIP, :], col[q], preferred_element_type=F32).astype(BF)
        begun[q] = jnp.dot(rows[:, 0:STRIP], part, preferred_element_type=F32)

    for n in (6, 7, 8):
        loads[n].wait()
    chosen = group[0]
    depth = jnp.float32(0.0)
    for g in range(4):
        depth = depth + jnp.where(chosen == g, defo[g], 0.0)
    depth = depth * jnp.float32(math.pi)
    k = lax.broadcasted_iota(jnp.int32, (KH, BLK), 0).astype(F32) / LROW
    angle = depth * (k * k) + 0.07
    ctf_s[...] = jnp.sin(angle)
    ctf_c[...] = jnp.cos(angle)

    arrive(ybuf, 2)
    fill = pltpu.make_async_copy(ybuf.at[c], tg.at[ty], lsem.at[6])
    fill.start()
    at = 3
    for dx in (1, 2, 3):
        xd = lax.rem(x + dx, 4)
        for core in (0, 1):
            for piece in (0, 1):
                src = tpl.at[core] if piece == 0 else ybuf.at[core]
                slot = t if piece == 0 else ty
                send(
                    src, tg.at[slot], at, 3 + (dx - 1) * 4 + c * 2 + piece,
                    (xd * 4 + yh * 2 + core, o),
                )
                at += 1
    send(tpl.at[other], tg.at[t], 15, 15, partner)
    send(ybuf.at[other], tg.at[ty], 16, 16, partner)

    told(1)
    tell(2)
    arrive(frame.at[pl.ds(STRIP, BLK)], 35)

    @pl.when(last)
    def _():
        inner[1].start()

    arrive(frame.at[pl.ds(STRIP + BLK, BLK)], 36)
    arrive(frame.at[pl.ds(2 * STRIP, BLK)], 37)
    keep1 = jnp.where(t < 15, 1.0, 0.0).astype(F32)
    keep2 = jnp.where(t < 14, 1.0, 0.0).astype(F32)
    row = lax.broadcasted_iota(jnp.int32, (TS, 2 * BLK), 0)
    keep = jnp.where(row < STRIP, keep1, keep2)

    def spectrum(q):
        part = jnp.dot(frame[STRIP:LROW, :], col[q], preferred_element_type=F32)
        part = (part * keep).astype(BF)
        real, imag = combine(
            begun[q] + jnp.dot(rows[:, STRIP:LROW], part, preferred_element_type=F32)
        )
        spec[q, :, 0:BLK] = real
        spec[q, :, BLK:] = imag
        return real * real + imag * imag

    for i in range(2):
        psend[i] = spectrum(2 * other + i).astype(BF)
        send(psend.at[i], precv.at[i], 17 + i, 17 + i, partner)

    for i in range(2):
        own = spectrum(2 * c + i)
        arrive(precv.at[i], 17 + i)
        own = own + precv[i].astype(F32)
        for n in range(CHIPS - 1):
            comb[i, n] = own[n * KC : (n + 1) * KC, :].astype(BF)
        comb[i, CHIPS - 1] = jnp.zeros((KC, BLK), BF)
        for d in FAR_FIRST:
            to = lax.rem(j + d, CHIPS)
            at = 39 + 7 * i + d
            send(comb.at[i, to], rsb.at[i, d - 1], at, at, near(to * 2 + c))
    told(2)
    tell(3)

    for dx in (1, 2, 3):
        xs = lax.rem(x + 4 - dx, 4)
        for core in (0, 1):
            for piece in (0, 1):
                row_of = yh if piece == 0 else 1 - yh
                arrive(tg.at[xs * 4 + row_of * 2 + core], 3 + (dx - 1) * 4 + core * 2 + piece)
    arrive(tg.at[j * 2 + other], 15)
    arrive(tg.at[x * 4 + (1 - yh) * 2 + other], 16)
    loads[5].wait()
    fill.wait()
    send(tg, tr, 19, 19, partner)

    for n, held in enumerate((tg, tr)):
        if n == 1:
            arrive(tr, 19)
        for s in range(16):
            tf[s * 24 : (s + 1) * 24, :] = held[s].astype(F32)
        values = tf[...]
        mean = jnp.sum(values) / (TS * TS)
        spread = jnp.sum(values * values) / (TS * TS) - mean * mean + 1e-05
        inverse = lax.rsqrt(jnp.full((1, 2 * BLK), spread, F32)) / (LROW * LCOL)
        rounded = values.astype(BF)
        for q in range(NQ):
            part = jnp.dot(rounded, col[q, 0:TS, :], preferred_element_type=F32)
            tspec[n, q] = ((part - mean * col_sum[q]) * inverse).astype(BF)

        i = n
        total = comb[i, j].astype(F32)
        for d in range(1, CHIPS):
            arrive(rsb.at[i, d - 1], 39 + 7 * i + d)
            total = total + rsb[i, d - 1].astype(F32)
        gall[c, i, j] = total.astype(BF)
        mine = gall.at[c, i, j]
        for d in FAR_FIRST:
            to = lax.rem(j + d, CHIPS)
            at = 53 + 7 * i + d
            send(mine, mine, at, at, near(to * 2 + c))
        send(mine, mine, 68 + 8 * i, 68 + 8 * i, partner)
    told(3)
    tell(4)

    for n in range(2):
        for q in range(NQ):
            real, imag = combine(
                jnp.dot(rows[:, 0:TS], tspec[n, q], preferred_element_type=F32)
            )
            hsp[n, q, :, 0:BLK] = real
            hsp[n, q, :, BLK:] = imag

    for i in range(2):
        for d in FAR_FIRST[::-1]:
            piece = gall.at[c, i, lax.rem(j + CHIPS - d, CHIPS)]
            arrive(piece, 53 + 7 * i + d)
            send(piece, piece, 68 + 8 * i + d, 68 + 8 * i + d, partner)
    for i in range(2):
        for d in range(CHIPS):
            arrive(gall.at[other, i, lax.rem(j + CHIPS - d, CHIPS)], 68 + 8 * i + d)

    def power(q):
        return jnp.concatenate([gall[q // 2, q % 2, n].astype(F32) for n in range(CHIPS)], 0)

    k = lax.broadcasted_iota(jnp.int32, (KP, BLK), 0)
    weight = jnp.where(k < LROW // 2, 2.0, 1.0) * jnp.where(k <= LROW // 2, 1.0, 0.0)
    weight = jnp.where(k == 0, 1.0, weight)
    summed = jnp.zeros((KP, BLK), F32)
    for q in range(NQ):
        summed = summed + power(q)
    average = jnp.sum(summed * weight) / (LROW * LCOL * 16.0)
    for q in range(NQ):
        lane = lax.broadcasted_iota(jnp.int32, (1, BLK), 1) + q * BLK
        lane = jnp.where(2 * lane < LCOL, lane, lane - LCOL).astype(F32) / LCOL
        phase = depth * (lane * lane)
        factor = -(ctf_s[...] * jnp.cos(phase) + ctf_c[...] * jnp.sin(phase))
        factor = factor * lax.rsqrt(power(q)[0:KH] / 16.0 + average)
        spec[q, :, 0:BLK] = spec[q, :, 0:BLK] * factor
        spec[q, :, BLK:] = spec[q, :, BLK:] * factor
    loads[3].wait()
    loads[4].wait()
    told(4)

    def a2a(d):
        to = lax.rem(o + d, 32)
        return remote(sbuf.at[to], rbuf.at[o], asem.at[d], bsem.at[d], (t, to))

    for n in range(2):
        for q in range(NQ):
            real, imag = spec[q, :, 0:BLK], spec[q, :, BLK:]
            h_re, h_im = hsp[n, q, :, 0:BLK], hsp[n, q, :, BLK:]
            qb[n, :, q * 256 : q * 256 + BLK] = (real * h_re + imag * h_im).astype(BF)
            qb[n, :, q * 256 + BLK : (q + 1) * 256] = (imag * h_re - real * h_im).astype(BF)
        y = jnp.dot(qb[n], back[...], preferred_element_type=F32).astype(BF)
        ys[0:KH, n * BLK : (n + 1) * BLK] = y[:, 0:BLK]
        ys[KH:, n * BLK : (n + 1) * BLK] = y[:, BLK:]
    score = jnp.dot(outt[...], ys[...], preferred_element_type=F32)
    for r in range(32):
        block = score[r * 8 : (r + 1) * 8, :]
        sbuf[r] = jnp.concatenate([block[:, 0:BLK], block[:, BLK:]], 0).astype(BF)

    for i in range(31):
        a2a(16 + (i + 1) // 2 * (1 - 2 * (i % 2))).start()
    own_rows = pltpu.make_async_copy(sbuf.at[o], rbuf.at[o], lsem.at[7])
    own_rows.start()

    def a2a_wait(d):
        src = lax.rem(o + 32 - d, 32)
        remote(rbuf.at[src], rbuf.at[src], asem.at[d], bsem.at[d], partner).wait_recv()

    for copy in started:
        copy.wait_send()

    @pl.when(last)
    def _():
        for copy in inner:
            copy.wait_send()

    own_rows.wait()
    for d in range(1, 32):
        a2a_wait(d)
    best = jnp.full((8, BLK), -jnp.inf, F32)
    first = jnp.zeros((8, BLK), F32)
    second = jnp.zeros((8, BLK), F32)
    for r in range(32):
        pair = rbuf[r].astype(F32)
        a, b = pair[0:8], pair[8:16]
        best = jnp.maximum(best, jnp.maximum(a, b))
        first = first + (a + b)
        second = second + (a * a + b * b)
    mean = first / 64.0
    spread = second / 64.0 - mean * mean
    res_o[0:8] = best
    res_o[8:16] = (best - mean) / jnp.sqrt(spread + 1e-05)
    for d in range(1, 32):
        a2a(d).wait_send()


def local(consts, micrograph, templates, defocus, group_of_tile):
    rows, col, back, out, col_sum = consts
    hbm = pl.BlockSpec(memory_space=pltpu.HBM)
    vmem = pl.BlockSpec(memory_space=pltpu.VMEM)
    v = pltpu.VMEM
    both = pl.pallas_call(
        kernel,
        out_shape=pltpu.VMEM((16, OUTC), F32),
        in_specs=[hbm] * 9,
        out_specs=vmem,
        scratch_shapes=[
            v((2 * KH, LROW), BF),
            v((NQ, LCOL, 2 * BLK), BF),
            v((2 * LCOL, 2 * OUTC), BF),
            v((STRIP, 2 * KH), BF),
            pltpu.SMEM((4,), F32),
            pltpu.SMEM((1,), jnp.int32),
            v((NQ, 1, 2 * BLK), F32),
            v((LROW, LCOL), BF),
            v((NQ, 2 * KH, 2 * BLK), F32),
            v((NQ, KH, 2 * BLK), F32),
            v((2, 24, TS), BF),
            v((16, 24, TS), BF),
            v((16, 24, TS), BF),
            v((TS, TS), F32),
            v((2, NQ, TS, 2 * BLK), BF),
            v((2, NQ, KH, 2 * BLK), F32),
            v((2, KH, BLK), BF),
            v((2, KH, BLK), BF),
            v((2, CHIPS, KC, BLK), BF),
            v((2, CHIPS - 1, KC, BLK), BF),
            v((2, 2, CHIPS, KC, BLK), BF),
            v((KH, BLK), F32),
            v((KH, BLK), F32),
            v((2, KH, 2 * LCOL), BF),
            v((2 * KH, 2 * BLK), BF),
            v((32, 16, BLK), BF),
            v((32, 16, BLK), BF),
            pltpu.SemaphoreType.DMA((12,)),
            pltpu.SemaphoreType.DMA((84,)),
            pltpu.SemaphoreType.DMA((84,)),
            pltpu.SemaphoreType.DMA((32,)),
            pltpu.SemaphoreType.DMA((32,)),
            pltpu.SemaphoreType.REGULAR((4,)),
        ],
        compiler_params=pltpu.CompilerParams(collective_id=0, has_side_effects=True),
        name="match",
    )(micrograph, templates, defocus, group_of_tile, rows, col, back, out, col_sum)
    return both[0:8], both[8:16]


def solution(mesh):
    consts = tuple(jnp.asarray(a) for a in tables())
    return jax.shard_map(
        functools.partial(local, consts),
        mesh=mesh,
        in_specs=(P("tile", None), P("orient", "tile", None), P(), P("tile")),
        out_specs=(P(("tile", "orient"), None),) * 2,
        check_vma=False,
    )
```
